512 devices in a mesh: seq: 64 (over z, x, core), head: 8 (over y).
Axes of the slice: x: 4, y: 8, z: 8, core: 2. Of those that a mesh axis runs over, the one named last changes fastest.
Arguments:
- queries: bfloat16 [24576, 5120], P(('seq', 'head')), may hold values from -6 to 6
- keys: bfloat16 [24576, 1024], P(('seq', 'head')), may hold values from -6 to 6
- values: bfloat16 [24576, 1024], P(('seq', 'head')), may hold values from -6 to 6
- outputs: bfloat16 [24576, 5120], P(('seq', 'head')), may hold values from -2 to 2
- output_gradient: bfloat16 [24576, 5120], P(('seq', 'head')), may hold values from -6 to 6
- lse: bfloat16 [24576, 40], P(('seq', 'head'))
- ranks: int32 [24576], P(('seq', 'head')), may hold values from 0 to 8192, as said below
Outputs:
- query_grads: bfloat16 [24576, 5120], P(('seq', 'head'))
- key_gradient_output: bfloat16 [24576, 1024], P(('seq', 'head'))
- value_gradient: bfloat16 [24576, 1024], P(('seq', 'head'))
The draws below stay inside these ranges and needn't reach their ends.
Inputs may be any that keep to these rules, and one draw needn't show every extreme that they name: Home shard s holds slots s * 384 to (s + 1) * 384 - 1. Its live slots are its first c_s slots, with 1 <= c_s <= 384, holding the consecutive ranks P_s, P_s + 1, ..., where P_s is the number of survivors of the shards before s; its other slots hold 8192. One shard holds exactly 384 survivors; all shards together 8192.
All inputs are finite; a program needn't handle non-finite values.
Results may differ from the reference program's by a relative error of at most 0.0056.
Values may be sent and summed in bfloat16 or wider, within the bound.
A program may use at most 64 MiB of HBM per device.

```python
import jax
import jax.numpy as jnp
from jax import lax

QUERY_HEADS = 40
KEY_VALUE_HEADS = 8
HEAD_SIZE = 128
BALANCED_TOKENS = 128
SHARD_CAPACITY = 384
N_SEQ = 64


def surviving_counts(key):
    base = jax.random.fold_in(key, 101)
    biggest = jax.random.randint(jax.random.fold_in(base, 1), (), 0, N_SEQ)
    weights = jax.random.randint(jax.random.fold_in(base, 2), (N_SEQ,), 50, 101)
    shard = jnp.arange(N_SEQ, dtype=jnp.int32)
    others = shard != biggest
    weights = jnp.where(others, weights, 0)
    removal = 2 * BALANCED_TOKENS * weights // jnp.sum(weights)
    remaining = 2 * BALANCED_TOKENS - jnp.sum(removal)
    order = jnp.cumsum(others.astype(jnp.int32)) - 1
    extra = (others & (order < remaining)).astype(jnp.int32)
    count_table = jnp.where(others, BALANCED_TOKENS - removal - extra, 3 * BALANCED_TOKENS)
    return count_table.astype(jnp.int32)


def draw_ranks(key, part):
    count_table = surviving_counts(key)
    starts = jnp.cumsum(count_table) - count_table
    within = jnp.arange(3 * BALANCED_TOKENS, dtype=jnp.int32)
    alive = within[None, :] < count_table[:, None]
    result = jnp.where(alive, starts[:, None] + within[None, :], BALANCED_TOKENS * N_SEQ)
    return result.reshape(-1).astype(jnp.int32)


def draw_lse(key, part):
    ranks = draw_ranks(key, part)
    surviving_tokens = BALANCED_TOKENS * N_SEQ
    tree_level = 0.5 * jnp.log(jnp.minimum(ranks, surviving_tokens - 1).astype(jnp.float32) + 1.0)
    noise_key = jax.random.fold_in(key, 202)
    noise = jax.random.uniform(noise_key, (ranks.shape[0], QUERY_HEADS), jnp.float32, 0.0, 1.0)
    return (tree_level[:, None] + noise).astype(jnp.bfloat16)


def block_scale(key, extent, split, smallest, largest):
    def one(axis_at, parts):
        heights = jax.random.uniform(jax.random.fold_in(jax.random.fold_in(key, 6), axis_at), (parts,), jnp.float32, smallest / len(split), largest / len(split))
        return jnp.repeat(jnp.exp(heights), extent[axis_at] // parts).reshape((-1,) + (1,) * (len(extent) - axis_at - 1))

    gain = one(*split[0])
    for cut in split[1:]:
        gain = gain * one(*cut)
    return gain


def centred(stream_key, shape, spread, limit, pieces=(), held_as=jnp.bfloat16):
    factor_of = block_scale(stream_key, shape, pieces, -0.22, 0.18) if pieces else 1.0
    values = jax.random.normal(stream_key, shape, jnp.float32) * spread * factor_of
    return jnp.minimum(jnp.maximum(values, -limit), limit).astype(held_as)


def setup_inputs(seed: int = 0) -> dict:
    splits = jax.random.split(jax.random.key(seed), 8)
    queries = centred(splits[0], (N_SEQ * SHARD_CAPACITY, QUERY_HEADS * HEAD_SIZE), 1.0, 6.0, ((0, 512),))
    keys = centred(splits[1], (N_SEQ * SHARD_CAPACITY, KEY_VALUE_HEADS * HEAD_SIZE), 1.0, 6.0, ((0, 512),))
    values = centred(splits[2], (N_SEQ * SHARD_CAPACITY, KEY_VALUE_HEADS * HEAD_SIZE), 1.0, 6.0, ((0, 512),))
    outputs = centred(splits[3], (N_SEQ * SHARD_CAPACITY, QUERY_HEADS * HEAD_SIZE), 0.3, 2.0, ((0, 512),))
    output_gradient = centred(splits[4], (N_SEQ * SHARD_CAPACITY, QUERY_HEADS * HEAD_SIZE), 1.0, 6.0, ((0, 512),))
    lse = draw_lse(jax.random.fold_in(splits[7], 71), 0)
    ranks = draw_ranks(jax.random.fold_in(splits[7], 71), 0)
    return dict(queries=queries, keys=keys, values=values, outputs=outputs, output_gradient=output_gradient, lse=lse, ranks=ranks)


def head_backward(args):
    query_g, key_gradient, value_g, grad_g, lse_g, delta_g = args
    surviving_tokens = key_gradient.shape[0]
    scale = HEAD_SIZE ** -0.5
    key_f = key_gradient.astype(jnp.float32)
    value_f = value_g.astype(jnp.float32)
    key_owner_rank = jnp.arange(surviving_tokens, dtype=jnp.int32)
    block_list = surviving_tokens // 512
    group_size = query_g.shape[1]
    query_b = query_g.reshape(block_list, 512, group_size, HEAD_SIZE)
    grad_b = grad_g.reshape(block_list, 512, group_size, HEAD_SIZE)
    lse_b = lse_g.reshape(block_list, 512, group_size)
    delta_b = delta_g.reshape(block_list, 512, group_size)

    def step(carry, inputs):
        key_accumulator, value_accumulator = carry
        query_blk, grad_blk, lse_blk, delta_blk, block_index = inputs
        query_rank = block_index * 512 + jnp.arange(512, dtype=jnp.int32)
        query_f = query_blk.astype(jnp.float32)
        grad_f = grad_blk.astype(jnp.float32)
        scores = jnp.einsum("qmc,kc->mqk", query_f, key_f) * scale
        mask = key_owner_rank[None, None, :] <= query_rank[None, :, None]
        probs = jnp.where(mask, jnp.exp(scores - lse_blk.astype(jnp.float32).T[:, :, None]), 0.0)
        dprob = jnp.einsum("qmc,kc->mqk", grad_f, value_f)
        dscore = probs * (dprob - delta_blk.astype(jnp.float32).T[:, :, None])
        probs_low = lax.optimization_barrier(probs.astype(jnp.bfloat16)).astype(jnp.float32)
        dscore_low = lax.optimization_barrier(dscore.astype(jnp.bfloat16)).astype(jnp.float32)
        query_result = scale * jnp.einsum("mqk,kc->qmc", dscore_low, key_f)
        key_accumulator = key_accumulator + scale * jnp.einsum("mqk,qmc->kc", dscore_low, query_f)
        value_accumulator = value_accumulator + jnp.einsum("mqk,qmc->kc", probs_low, grad_f)
        return (key_accumulator, value_accumulator), query_result

    zero_fill = jnp.zeros((surviving_tokens, HEAD_SIZE), jnp.float32)
    (key_accumulator, value_accumulator), query_result = lax.scan(
        step, (zero_fill, zero_fill), (query_b, grad_b, lse_b, delta_b, jnp.arange(block_list, dtype=jnp.int32)))
    return query_result.reshape(surviving_tokens, group_size, HEAD_SIZE), key_accumulator, value_accumulator


def reference(queries, keys, values, outputs, output_gradient, lse, ranks):
    surviving_tokens = BALANCED_TOKENS * N_SEQ
    row_total = ranks.shape[0]
    group_size = QUERY_HEADS // KEY_VALUE_HEADS
    target_rank = jnp.where(ranks < surviving_tokens, ranks, surviving_tokens).astype(jnp.int32)
    slot_index = jnp.zeros((surviving_tokens,), jnp.int32).at[target_rank].set(
        jnp.arange(row_total, dtype=jnp.int32), mode="drop")
    query_shard = queries[slot_index].reshape(surviving_tokens, KEY_VALUE_HEADS, group_size, HEAD_SIZE)
    key_shard = keys[slot_index].reshape(surviving_tokens, KEY_VALUE_HEADS, HEAD_SIZE)
    value_shard = values[slot_index].reshape(surviving_tokens, KEY_VALUE_HEADS, HEAD_SIZE)
    gradient_shard = output_gradient[slot_index].reshape(surviving_tokens, KEY_VALUE_HEADS, group_size, HEAD_SIZE)
    output_shard = outputs[slot_index].reshape(surviving_tokens, KEY_VALUE_HEADS, group_size, HEAD_SIZE)
    logsumexp_shard = lse[slot_index].reshape(surviving_tokens, KEY_VALUE_HEADS, group_size)
    delta_s = jnp.sum(gradient_shard.astype(jnp.float32) * output_shard.astype(jnp.float32), axis=-1).astype(jnp.bfloat16)
    query_result, key_result, value_result = lax.map(head_backward, (
        query_shard.transpose(1, 0, 2, 3), key_shard.transpose(1, 0, 2), value_shard.transpose(1, 0, 2),
        gradient_shard.transpose(1, 0, 2, 3), logsumexp_shard.transpose(1, 0, 2), delta_s.transpose(1, 0, 2)))
    query_row_block = query_result.transpose(1, 0, 2, 3).reshape(surviving_tokens, QUERY_HEADS * HEAD_SIZE).astype(jnp.bfloat16)
    key_row_block = key_result.transpose(1, 0, 2).reshape(surviving_tokens, KEY_VALUE_HEADS * HEAD_SIZE).astype(jnp.bfloat16)
    value_row_block = value_result.transpose(1, 0, 2).reshape(surviving_tokens, KEY_VALUE_HEADS * HEAD_SIZE).astype(jnp.bfloat16)
    query_grads = jnp.zeros((row_total, QUERY_HEADS * HEAD_SIZE), jnp.bfloat16).at[slot_index].set(query_row_block)
    key_gradient_output = jnp.zeros((row_total, KEY_VALUE_HEADS * HEAD_SIZE), jnp.bfloat16).at[slot_index].set(key_row_block)
    value_gradient = jnp.zeros((row_total, KEY_VALUE_HEADS * HEAD_SIZE), jnp.bfloat16).at[slot_index].set(value_row_block)
    return (query_grads, key_gradient_output, value_gradient)
```

```python
import functools

import jax
import jax.numpy as jnp
from jax import lax
from jax.experimental import pallas as pl
from jax.experimental.pallas import tpu as pltpu
from jax.sharding import PartitionSpec as P

QUERY_HEADS = 40
KEY_VALUE_HEADS = 8
HEAD_SIZE = 128
BALANCED_TOKENS = 128
GROUP = QUERY_HEADS // KEY_VALUE_HEADS
LOG2E = 1.4426950408889634
ROWS = 128
BAND = 16
OWNERS = 16


def attention_kernel(
    meta_ref, qd_ref, lse_ref, delta_ref, kv_ref, dq_ref, dkv_ref, q_sc, g_sc, dq_sc, acc
):
    first = meta_ref[0]
    count = meta_ref[1]
    owners = kv_ref.shape[0]
    blocks = q_sc.shape[0]
    stacked = GROUP * ROWS
    chunk = OWNERS * BAND
    scale = HEAD_SIZE ** (-0.5)
    row_span = BAND * owners
    acc[...] = jnp.zeros_like(acc)
    dq_sc[...] = jnp.zeros_like(dq_sc)
    for b in range(blocks):
        live = (lax.broadcasted_iota(jnp.int32, (ROWS, HEAD_SIZE), 0) + b * ROWS) < count
        for m in range(GROUP):
            rows = pl.ds(b * ROWS, ROWS)
            q = qd_ref[rows, pl.ds(m * HEAD_SIZE, HEAD_SIZE)]
            g = qd_ref[rows, pl.ds((GROUP + m) * HEAD_SIZE, HEAD_SIZE)]
            zero = jnp.zeros((), jnp.float32)
            q_sc[b, pl.ds(m * ROWS, ROWS), :] = jnp.where(
                live, q.astype(jnp.float32), zero
            ).astype(jnp.bfloat16)
            g_sc[b, pl.ds(m * ROWS, ROWS), :] = jnp.where(
                live, g.astype(jnp.float32), zero
            ).astype(jnp.bfloat16)
    live_blocks = (count + ROWS - 1) // ROWS
    key_blocks = (first + count + row_span - 1) // row_span
    index = lax.broadcasted_iota(jnp.int32, (chunk, stacked), 0)
    key_local = (index % BAND) * owners + index // BAND
    row_local = lax.broadcasted_iota(jnp.int32, (chunk, stacked), 1) % ROWS
    gap = key_local - row_local

    def key_block(j, carry):
        lowest = jnp.maximum(j * row_span - first, 0) // ROWS
        band = pl.ds(pl.multiple_of(j * BAND, BAND), BAND)
        for c in range(owners // OWNERS):
            own = pl.ds(c * OWNERS, OWNERS)
            key = kv_ref[own, band, pl.ds(0, HEAD_SIZE)].reshape(chunk, HEAD_SIZE)
            value = kv_ref[own, band, pl.ds(HEAD_SIZE, HEAD_SIZE)].reshape(chunk, HEAD_SIZE)
            key_t = key.astype(jnp.float32).T.astype(jnp.bfloat16)

            def row_block(b, inner):
                q = q_sc[b]
                g = g_sc[b]
                nt = (((1,), (1,)), ((), ()))
                nn = (((1,), (0,)), ((), ()))
                f32 = jnp.float32
                score = lax.dot_general(key, q, nt, preferred_element_type=f32)
                dprob = lax.dot_general(value, g, nt, preferred_element_type=f32)
                limit = first + b * ROWS - j * row_span - c * OWNERS
                prob = jnp.where(
                    gap <= limit,
                    jnp.exp2(score * (scale * LOG2E) - lse_ref[pl.ds(b, 1), :]),
                    0.0,
                )
                dscore = prob * (dprob - delta_ref[pl.ds(b, 1), :])
                prob_low = prob.astype(jnp.bfloat16)
                dscore_low = dscore.astype(jnp.bfloat16)
                dk = lax.dot_general(dscore_low, q, nn, preferred_element_type=f32)
                dv = lax.dot_general(prob_low, g, nn, preferred_element_type=f32)
                acc[own, band, pl.ds(0, HEAD_SIZE)] += dk.reshape(OWNERS, BAND, HEAD_SIZE)
                acc[own, band, pl.ds(HEAD_SIZE, HEAD_SIZE)] += dv.reshape(OWNERS, BAND, HEAD_SIZE)
                dq_sc[b] += lax.dot_general(key_t, dscore_low, nn, preferred_element_type=f32)
                return inner

            lax.fori_loop(lowest, live_blocks, row_block, 0)
        return carry

    lax.fori_loop(0, key_blocks, key_block, 0)
    for b in range(blocks):
        for m in range(GROUP):
            part = dq_sc[b, :, pl.ds(m * ROWS, ROWS)].T * scale
            dq_ref[pl.ds(b * ROWS, ROWS), pl.ds(m * HEAD_SIZE, HEAD_SIZE)] = part.astype(
                dq_ref.dtype
            )
    dkv_ref[:, :, pl.ds(0, HEAD_SIZE)] = (acc[:, :, pl.ds(0, HEAD_SIZE)] * scale).astype(
        dkv_ref.dtype
    )
    dkv_ref[:, :, pl.ds(HEAD_SIZE, HEAD_SIZE)] = acc[:, :, pl.ds(HEAD_SIZE, HEAD_SIZE)].astype(
        dkv_ref.dtype
    )


def attention(meta, qd, lse, delta, kv, interpret=False):
    capacity = qd.shape[0]
    owners, per_owner, width = kv.shape
    blocks = capacity // ROWS
    vmem = pl.BlockSpec(memory_space=pltpu.VMEM)
    return pl.pallas_call(
        attention_kernel,
        name="attention",
        out_shape=(
            jax.ShapeDtypeStruct((capacity, GROUP * HEAD_SIZE), jnp.bfloat16),
            jax.ShapeDtypeStruct(kv.shape, jnp.bfloat16),
        ),
        in_specs=[pl.BlockSpec(memory_space=pltpu.SMEM), vmem, vmem, vmem, vmem],
        out_specs=(vmem, vmem),
        scratch_shapes=[
            pltpu.VMEM((blocks, GROUP * ROWS, HEAD_SIZE), jnp.bfloat16),
            pltpu.VMEM((blocks, GROUP * ROWS, HEAD_SIZE), jnp.bfloat16),
            pltpu.VMEM((blocks, HEAD_SIZE, GROUP * ROWS), jnp.float32),
            pltpu.VMEM(kv.shape, jnp.float32),
        ],
        compiler_params=pltpu.CompilerParams(vmem_limit_bytes=56 << 20),
        cost_estimate=pl.CostEstimate(
            flops=10 * capacity * GROUP * HEAD_SIZE * owners * per_owner // 2,
            bytes_accessed=2 * (2 * kv.size + 3 * qd.size),
            transcendentals=0,
        ),
        interpret=interpret,
    )(meta, qd, lse, delta, kv)


def per_device(queries, keys, values, outputs, output_gradient, lse, ranks):
    owners = lax.axis_size("seq")
    heads = lax.axis_size("head")
    me = lax.axis_index("seq")
    home_rows = queries.shape[0]
    capacity = home_rows * heads
    slots = capacity // owners
    survivors = BALANCED_TOKENS * owners
    bf16 = jnp.bfloat16
    width = 2 * HEAD_SIZE
    exchange = functools.partial(lax.all_to_all, split_axis=0, concat_axis=0, tiled=True)

    dots = jnp.sum(
        output_gradient.astype(jnp.float32).reshape(home_rows, QUERY_HEADS, HEAD_SIZE)
        * outputs.astype(jnp.float32).reshape(home_rows, QUERY_HEADS, HEAD_SIZE),
        axis=-1,
    ).astype(bf16)

    def by_head(array):
        return array.reshape(home_rows, heads, -1).transpose(1, 0, 2)

    living = jnp.sum((ranks < survivors).astype(jnp.int32))
    digits = jnp.stack([ranks[0] // 128, ranks[0] % 128, living]).astype(bf16)
    small = jnp.concatenate([by_head(lse), by_head(dots)], axis=-1).transpose(0, 2, 1)
    small = jnp.pad(small, ((0, 0), (0, 0), (0, width - home_rows)))
    digit_rows = jnp.broadcast_to(
        jnp.pad(digits, (0, width - 3))[None, None], (heads, 16 - 2 * GROUP, width)
    )
    first_pack = jnp.concatenate(
        [jnp.concatenate([by_head(keys), by_head(values)], axis=-1), small, digit_rows], axis=1
    )
    first_pack = exchange(first_pack, "head")
    pairs = first_pack[:, :home_rows].reshape(slots, owners, width)
    extra = first_pack[:, home_rows:].astype(jnp.float32)
    first_rank = (extra[0, 2 * GROUP, 0] * 128 + extra[0, 2 * GROUP, 1]).astype(jnp.int32)
    count = jnp.sum(extra[:, 2 * GROUP, 2]).astype(jnp.int32)

    turn = first_rank % owners
    by_owner = pairs.transpose(1, 0, 2)
    by_owner = lax.dynamic_slice_in_dim(
        jnp.concatenate([by_owner, by_owner], axis=0), owners - turn, owners, 0
    )
    head_digits = jnp.stack(
        [first_rank // 128, first_rank % 128, count // 128, count % 128]
    ).astype(bf16)
    tail = jnp.broadcast_to(
        jnp.pad(head_digits, (0, width - 4))[None, None], (owners, 8 - slots, width)
    )
    arrived = exchange(jnp.concatenate([by_owner, tail], axis=1), "seq")
    told = arrived[:, slots].astype(jnp.float32)
    starts = (told[:, 0] * 128 + told[:, 1]).astype(jnp.int32)
    counts = (told[:, 2] * 128 + told[:, 3]).astype(jnp.int32)
    within = jnp.arange(8, dtype=jnp.int32)[None, :] * owners + ((me - starts) % owners)[:, None]
    alive = (within < counts[:, None]) & (jnp.arange(8) < slots)[None, :]
    target = jnp.where(alive, (starts[:, None] + within) // owners, -1).reshape(-1)
    pick = (target[None, :] == jnp.arange(BALANCED_TOKENS, dtype=jnp.int32)[:, None]).astype(bf16)
    placed = jnp.dot(
        pick, arrived.reshape(owners * 8, width), preferred_element_type=jnp.float32
    ).astype(bf16)
    all_kv = lax.all_gather(placed, "seq", axis=0, tiled=False)

    placed_first, queries, output_gradient = lax.optimization_barrier(
        (placed, queries, output_gradient)
    )
    qd = exchange(
        jnp.concatenate([by_head(queries), by_head(output_gradient)], axis=-1), "head"
    ).reshape(capacity, 2 * GROUP * HEAD_SIZE)

    slot = jnp.arange(capacity, dtype=jnp.int32)
    per_row = extra[:, : 2 * GROUP, :home_rows].transpose(1, 0, 2).reshape(2 * GROUP, capacity)
    per_row = jnp.where(slot[None, :] < count, per_row, 0.0)
    per_row = per_row.reshape(2, GROUP, capacity // ROWS, ROWS).transpose(0, 2, 1, 3)
    per_row = per_row.reshape(2, capacity // ROWS, GROUP * ROWS)
    dq, dkv = attention(
        jnp.stack([first_rank, count]), qd, per_row[0] * LOG2E, per_row[1], all_kv
    )

    parts = exchange(dkv, "seq")
    summed = jnp.sum(parts.astype(jnp.float32), axis=0).astype(bf16)
    back = lax.dot_general(
        pick, summed, (((0,), (0,)), ((), ())), preferred_element_type=jnp.float32
    ).astype(bf16)
    back = exchange(back.reshape(owners, 8, width), "seq")
    back = lax.dynamic_slice_in_dim(jnp.concatenate([back, back], axis=0), turn, owners, 0)
    back = back[:, :slots].transpose(1, 0, 2).reshape(heads, home_rows, width)
    back = exchange(back, "head")
    dq = exchange(dq.reshape(heads, home_rows, GROUP * HEAD_SIZE), "head")
    query_grads = dq.transpose(1, 0, 2).reshape(home_rows, -1)
    key_grads = back[:, :, :HEAD_SIZE].transpose(1, 0, 2).reshape(home_rows, -1)
    value_grads = back[:, :, HEAD_SIZE:].transpose(1, 0, 2).reshape(home_rows, -1)
    return (query_grads, key_grads, value_grads)


def solution(mesh):
    placed = P(("seq", "head"), None)
    return jax.shard_map(
        per_device,
        mesh=mesh,
        in_specs=(placed,) * 6 + (P(("seq", "head")),),
        out_specs=(placed,) * 3,
        check_vma=False,
    )
```

```python
import functools

import jax
import jax.numpy as jnp
from jax import lax
from jax.experimental import pallas as pl
from jax.experimental.pallas import tpu as pltpu
from jax.sharding import PartitionSpec as P

QUERY_HEADS = 40
KEY_VALUE_HEADS = 8
HEAD_SIZE = 128
BALANCED_TOKENS = 128
GROUP = QUERY_HEADS // KEY_VALUE_HEADS
LOG2E = 1.4426950408889634
ROWS = 128
BAND = 16
OWNERS = 16


def attention_kernel(
    meta_ref, qd_ref, lse_ref, delta_ref, kv_ref, dq_ref, dkv_ref, q_sc, g_sc, dq_sc, acc
):
    first = meta_ref[0]
    count = meta_ref[1]
    owners = kv_ref.shape[0]
    blocks = q_sc.shape[0]
    stacked = GROUP * ROWS
    chunk = OWNERS * BAND
    scale = HEAD_SIZE ** (-0.5)
    row_span = BAND * owners
    acc[...] = jnp.zeros_like(acc)
    dq_sc[...] = jnp.zeros_like(dq_sc)
    for b in range(blocks):
        live = (lax.broadcasted_iota(jnp.int32, (ROWS, HEAD_SIZE), 0) + b * ROWS) < count
        for m in range(GROUP):
            rows = pl.ds(b * ROWS, ROWS)
            q = qd_ref[rows, pl.ds(m * HEAD_SIZE, HEAD_SIZE)]
            g = qd_ref[rows, pl.ds((GROUP + m) * HEAD_SIZE, HEAD_SIZE)]
            zero = jnp.zeros((), jnp.float32)
            q_sc[b, pl.ds(m * ROWS, ROWS), :] = jnp.where(
                live, q.astype(jnp.float32), zero
            ).astype(jnp.bfloat16)
            g_sc[b, pl.ds(m * ROWS, ROWS), :] = jnp.where(
                live, g.astype(jnp.float32), zero
            ).astype(jnp.bfloat16)
    live_blocks = (count + ROWS - 1) // ROWS
    key_blocks = (first + count + row_span - 1) // row_span
    index = lax.broadcasted_iota(jnp.int32, (chunk, stacked), 0)
    place_in = index // BAND
    key_local = (index % BAND) * owners + (place_in // 4) * 8 + (place_in % 4) * 2
    row_local = lax.broadcasted_iota(jnp.int32, (chunk, stacked), 1) % ROWS
    gap = key_local - row_local

    def key_block(j, carry):
        lowest = jnp.maximum(j * row_span - first, 0) // ROWS
        band = pl.ds(pl.multiple_of(j * BAND, BAND), BAND)
        for c in range(owners // OWNERS):
            own = pl.ds(c * OWNERS, OWNERS)
            key = kv_ref[own, band, pl.ds(0, HEAD_SIZE)].reshape(chunk, HEAD_SIZE)
            value = kv_ref[own, band, pl.ds(HEAD_SIZE, HEAD_SIZE)].reshape(chunk, HEAD_SIZE)
            key_t = key.astype(jnp.float32).T.astype(jnp.bfloat16)

            def row_block(b, inner):
                q = q_sc[b]
                g = g_sc[b]
                nt = (((1,), (1,)), ((), ()))
                nn = (((1,), (0,)), ((), ()))
                f32 = jnp.float32
                score = lax.dot_general(key, q, nt, preferred_element_type=f32)
                dprob = lax.dot_general(value, g, nt, preferred_element_type=f32)
                limit = first + b * ROWS - j * row_span - (c % 2) * 32 - c // 2
                prob = jnp.where(
                    gap <= limit,
                    jnp.exp2(score * (scale * LOG2E) - lse_ref[pl.ds(b, 1), :]),
                    0.0,
                )
                dscore = prob * (dprob - delta_ref[pl.ds(b, 1), :])
                prob_low = prob.astype(jnp.bfloat16)
                dscore_low = dscore.astype(jnp.bfloat16)
                dk = lax.dot_general(dscore_low, q, nn, preferred_element_type=f32)
                dv = lax.dot_general(prob_low, g, nn, preferred_element_type=f32)
                acc[own, band, pl.ds(0, HEAD_SIZE)] += dk.reshape(OWNERS, BAND, HEAD_SIZE)
                acc[own, band, pl.ds(HEAD_SIZE, HEAD_SIZE)] += dv.reshape(OWNERS, BAND, HEAD_SIZE)
                dq_sc[b] += lax.dot_general(key_t, dscore_low, nn, preferred_element_type=f32)
                return inner

            lax.fori_loop(lowest, live_blocks, row_block, 0)
        return carry

    lax.fori_loop(0, key_blocks, key_block, 0)
    for b in range(blocks):
        for m in range(GROUP):
            part = dq_sc[b, :, pl.ds(m * ROWS, ROWS)].T * scale
            dq_ref[pl.ds(b * ROWS, ROWS), pl.ds(m * HEAD_SIZE, HEAD_SIZE)] = part.astype(
                dq_ref.dtype
            )
    dkv_ref[:, :, pl.ds(0, HEAD_SIZE)] = (acc[:, :, pl.ds(0, HEAD_SIZE)] * scale).astype(
        dkv_ref.dtype
    )
    dkv_ref[:, :, pl.ds(HEAD_SIZE, HEAD_SIZE)] = acc[:, :, pl.ds(HEAD_SIZE, HEAD_SIZE)].astype(
        dkv_ref.dtype
    )


def attention(meta, qd, lse, delta, kv, interpret=False):
    capacity = qd.shape[0]
    owners, per_owner, width = kv.shape
    blocks = capacity // ROWS
    vmem = pl.BlockSpec(memory_space=pltpu.VMEM)
    return pl.pallas_call(
        attention_kernel,
        name="attention",
        out_shape=(
            jax.ShapeDtypeStruct((capacity, GROUP * HEAD_SIZE), jnp.bfloat16),
            jax.ShapeDtypeStruct(kv.shape, jnp.bfloat16),
        ),
        in_specs=[pl.BlockSpec(memory_space=pltpu.SMEM), vmem, vmem, vmem, vmem],
        out_specs=(vmem, vmem),
        scratch_shapes=[
            pltpu.VMEM((blocks, GROUP * ROWS, HEAD_SIZE), jnp.bfloat16),
            pltpu.VMEM((blocks, GROUP * ROWS, HEAD_SIZE), jnp.bfloat16),
            pltpu.VMEM((blocks, HEAD_SIZE, GROUP * ROWS), jnp.float32),
            pltpu.VMEM(kv.shape, jnp.float32),
        ],
        compiler_params=pltpu.CompilerParams(vmem_limit_bytes=56 << 20),
        cost_estimate=pl.CostEstimate(
            flops=10 * capacity * GROUP * HEAD_SIZE * owners * per_owner // 2,
            bytes_accessed=2 * (2 * kv.size + 3 * qd.size),
            transcendentals=0,
        ),
        interpret=interpret,
    )(meta, qd, lse, delta, kv)


def place(seq_index):
    return seq_index // 8, (seq_index // 2) % 4, seq_index % 2


def peers():
    seq = lax.axis_index("seq")
    head = lax.axis_index("head")
    z, x, core = place(seq)
    spot = lambda z, x, core: (z * 8 + x * 2 + core, head)
    to_z = [None] + [spot((z + d) % 8, x, core) for d in range(1, 8)]
    to_x = [None] + [spot(z, (x + e) % 4, core) for e in range(1, 4)]
    partner = spot(z, x, 1 - core)
    to_head = [None] + [(seq, (head + d) % 8) for d in range(1, 8)]
    return z, x, core, head, to_z, to_x, partner, to_head


def meet(groups):
    barrier = pltpu.get_barrier_semaphore()
    total = 0
    for group in groups:
        for device in group:
            pl.semaphore_signal(
                barrier, inc=1, device_id=device, device_id_type=pl.DeviceIdType.MESH
            )
            total += 1
    pl.semaphore_wait(barrier, total)


def remote(src, dst, send, recv, device):
    return pltpu.make_async_remote_copy(
        src_ref=src,
        dst_ref=dst,
        send_sem=send,
        recv_sem=recv,
        device_id=device,
        device_id_type=pl.DeviceIdType.MESH,
    )


NEAR_FIRST = (0, 1, 7, 2, 6, 3, 5, 4)


def gather_kernel(
    own_ref, qd_ref, kv_ref, rows_ref, own_sem, z_send, z_recv, x_send, x_recv, p_send, p_recv,
    h_send, h_recv,
):
    z, x, core, head, to_z, to_x, partner, to_head = peers()
    meet((to_z[1:], to_x[1:], (partner,), to_head[1:]))
    copies = []
    for d in NEAR_FIRST[1:]:
        copy = remote(own_ref, kv_ref.at[core, z, x], z_send.at[d], z_recv.at[d], to_z[d])
        copy.start()
        copies.append(copy)
    for d in NEAR_FIRST[1:]:
        copy = remote(
            qd_ref.at[(head + d) % 8], rows_ref.at[head], h_send.at[d], h_recv.at[d], to_head[d]
        )
        copy.start()
        copies.append(copy)
    mine = pltpu.make_async_copy(own_ref, kv_ref.at[core, z, x], own_sem.at[0])
    mine.start()
    kept = pltpu.make_async_copy(qd_ref.at[head], rows_ref.at[head], own_sem.at[1])
    kept.start()
    for d in NEAR_FIRST:
        source = (z + 8 - d) % 8
        block = kv_ref.at[core, source, x]
        if d == 0:
            mine.wait()
        else:
            remote(own_ref, block, z_send.at[d], z_recv.at[d], to_z[d]).wait_recv()
        for e in (1, 3, 2):
            copy = remote(block, block, x_send.at[d, e], x_recv.at[d, e], to_x[e])
            copy.start()
            copies.append(copy)
    for d in NEAR_FIRST:
        source = (z + 8 - d) % 8
        for e in (1, 3, 2):
            block = kv_ref.at[core, source, (x + 4 - e) % 4]
            remote(block, block, x_send.at[d, e], x_recv.at[d, e], to_x[e]).wait_recv()
        row = kv_ref.at[core, source]
        copy = remote(row, row, p_send.at[d], p_recv.at[d], partner)
        copy.start()
        copies.append(copy)
    for d in NEAR_FIRST:
        row = kv_ref.at[1 - core, (z + 8 - d) % 8]
        remote(row, row, p_send.at[d], p_recv.at[d], partner).wait_recv()
    for d in NEAR_FIRST[1:]:
        part = rows_ref.at[(head + 8 - d) % 8]
        remote(part, part, h_send.at[d], h_recv.at[d], to_head[d]).wait_recv()
    kept.wait()
    for copy in copies:
        copy.wait_send()


def gather(own, qd):
    vmem = pl.BlockSpec(memory_space=pltpu.VMEM)
    dma = pltpu.SemaphoreType.DMA
    return pl.pallas_call(
        gather_kernel,
        name="gather",
        out_shape=(
            jax.ShapeDtypeStruct((2, 8, 4) + own.shape, own.dtype),
            jax.ShapeDtypeStruct(qd.shape, qd.dtype),
        ),
        in_specs=[vmem, vmem],
        out_specs=(vmem, vmem),
        scratch_shapes=[
            dma((2,)), dma((8,)), dma((8,)), dma((8, 4)), dma((8, 4)), dma((8,)), dma((8,)),
            dma((8,)), dma((8,)),
        ],
        compiler_params=pltpu.CompilerParams(
            collective_id=0, has_side_effects=True, vmem_limit_bytes=32 << 20
        ),
    )(own, qd)


def reduce_kernel(
    kv_ref, dq_ref, sum_ref, rows_ref, from_core, to_row, from_row, to_column, from_column, total,
    own_sem, p_send, p_recv, x_send, x_recv, z_send, z_recv, h_send, h_recv,
):
    z, x, core, head, to_z, to_x, partner, to_head = peers()
    f32 = jnp.float32
    meet((to_z[1:], to_x[1:], (partner,), to_head[1:]))
    order = (4, 3, 5, 2, 6, 1, 7, 0)
    copies = []
    for d in order:
        there = (z + d) % 8
        copy = remote(
            kv_ref.at[1 - core, there], from_core.at[there], p_send.at[d], p_recv.at[d], partner
        )
        copy.start()
        copies.append(copy)
    for d in NEAR_FIRST[1:]:
        copy = remote(
            dq_ref.at[(head + d) % 8], rows_ref.at[head], h_send.at[d], h_recv.at[d], to_head[d]
        )
        copy.start()
        copies.append(copy)
    kept = pltpu.make_async_copy(dq_ref.at[head], rows_ref.at[head], own_sem.at[0])
    kept.start()
    for d in order:
        there = (z + d) % 8
        remote(
            kv_ref.at[1 - core, there], from_core.at[there], p_send.at[d], p_recv.at[d], partner
        ).wait_recv()
        for e in (2, 1, 3):
            other = (x + e) % 4
            to_row[e, d] = (
                kv_ref[core, there, other].astype(f32) + from_core[there, other].astype(f32)
            ).astype(to_row.dtype)
            copy = remote(
                to_row.at[e, d], from_row.at[e, d], x_send.at[e, d], x_recv.at[e, d], to_x[e]
            )
            copy.start()
            copies.append(copy)
    for d in order:
        there = (z + d) % 8
        part = kv_ref[core, there, x].astype(f32) + from_core[there, x].astype(f32)
        for e in (1, 3, 2):
            remote(
                to_row.at[e, d], from_row.at[e, d], x_send.at[e, d], x_recv.at[e, d], to_x[e]
            ).wait_recv()
            part = part + from_row[e, d].astype(f32)
        if d == 0:
            total[...] = part
        else:
            to_column[d] = part.astype(to_column.dtype)
            copy = remote(
                to_column.at[d], from_column.at[d], z_send.at[d], z_recv.at[d], to_z[d]
            )
            copy.start()
            copies.append(copy)
    part = total[...]
    for d in order[:-1]:
        remote(
            to_column.at[d], from_column.at[d], z_send.at[d], z_recv.at[d], to_z[d]
        ).wait_recv()
        part = part + from_column[d].astype(f32)
    sum_ref[...] = part.astype(sum_ref.dtype)
    for d in NEAR_FIRST[1:]:
        piece = rows_ref.at[(head + 8 - d) % 8]
        remote(piece, piece, h_send.at[d], h_recv.at[d], to_head[d]).wait_recv()
    kept.wait()
    for copy in copies:
        copy.wait_send()


def reduce(dkv, dq):
    vmem = pl.BlockSpec(memory_space=pltpu.VMEM)
    dma = pltpu.SemaphoreType.DMA
    block = dkv.shape[3:]
    bf16 = jnp.bfloat16
    return pl.pallas_call(
        reduce_kernel,
        name="reduce",
        out_shape=(
            jax.ShapeDtypeStruct(block, bf16),
            jax.ShapeDtypeStruct(dq.shape, dq.dtype),
        ),
        in_specs=[vmem, vmem],
        out_specs=(vmem, vmem),
        scratch_shapes=[
            pltpu.VMEM((8, 4) + block, bf16),
            pltpu.VMEM((4, 8) + block, bf16),
            pltpu.VMEM((4, 8) + block, bf16),
            pltpu.VMEM((8,) + block, bf16),
            pltpu.VMEM((8,) + block, bf16),
            pltpu.VMEM(block, jnp.float32),
            dma((1,)), dma((8,)), dma((8,)), dma((4, 8)), dma((4, 8)), dma((8,)), dma((8,)),
            dma((8,)), dma((8,)),
        ],
        compiler_params=pltpu.CompilerParams(
            collective_id=1, has_side_effects=True, vmem_limit_bytes=40 << 20
        ),
    )(dkv, dq)


def per_device(queries, keys, values, outputs, output_gradient, lse, ranks):
    owners = lax.axis_size("seq")
    heads = lax.axis_size("head")
    me = lax.axis_index("seq")
    home_rows = queries.shape[0]
    capacity = home_rows * heads
    slots = capacity // owners
    survivors = BALANCED_TOKENS * owners
    bf16 = jnp.bfloat16
    width = 2 * HEAD_SIZE
    exchange = functools.partial(lax.all_to_all, split_axis=0, concat_axis=0, tiled=True)

    dots = jnp.sum(
        output_gradient.astype(jnp.float32).reshape(home_rows, QUERY_HEADS, HEAD_SIZE)
        * outputs.astype(jnp.float32).reshape(home_rows, QUERY_HEADS, HEAD_SIZE),
        axis=-1,
    ).astype(bf16)

    def by_head(array):
        return array.reshape(home_rows, heads, -1).transpose(1, 0, 2)

    living = jnp.sum((ranks < survivors).astype(jnp.int32))
    digits = jnp.stack([ranks[0] // 128, ranks[0] % 128, living]).astype(bf16)
    small = jnp.concatenate([by_head(lse), by_head(dots)], axis=-1).transpose(0, 2, 1)
    small = jnp.pad(small, ((0, 0), (0, 0), (0, width - home_rows)))
    digit_rows = jnp.broadcast_to(
        jnp.pad(digits, (0, width - 3))[None, None], (heads, 16 - 2 * GROUP, width)
    )
    first_pack = jnp.concatenate(
        [jnp.concatenate([by_head(keys), by_head(values)], axis=-1), small, digit_rows], axis=1
    )
    first_pack = exchange(first_pack, "head")
    pairs = first_pack[:, :home_rows].reshape(slots, owners, width)
    extra = first_pack[:, home_rows:].astype(jnp.float32)
    first_rank = (extra[0, 2 * GROUP, 0] * 128 + extra[0, 2 * GROUP, 1]).astype(jnp.int32)
    count = jnp.sum(extra[:, 2 * GROUP, 2]).astype(jnp.int32)

    turn = first_rank % owners
    by_owner = pairs.transpose(1, 0, 2)
    by_owner = lax.dynamic_slice_in_dim(
        jnp.concatenate([by_owner, by_owner], axis=0), owners - turn, owners, 0
    )
    head_digits = jnp.stack(
        [first_rank // 128, first_rank % 128, count // 128, count % 128]
    ).astype(bf16)
    tail = jnp.broadcast_to(
        jnp.pad(head_digits, (0, width - 4))[None, None], (owners, 8 - slots, width)
    )
    arrived = exchange(jnp.concatenate([by_owner, tail], axis=1), "seq")
    told = arrived[:, slots].astype(jnp.float32)
    starts = (told[:, 0] * 128 + told[:, 1]).astype(jnp.int32)
    counts = (told[:, 2] * 128 + told[:, 3]).astype(jnp.int32)
    within = jnp.arange(8, dtype=jnp.int32)[None, :] * owners + ((me - starts) % owners)[:, None]
    alive = (within < counts[:, None]) & (jnp.arange(8) < slots)[None, :]
    target = jnp.where(alive, (starts[:, None] + within) // owners, -1).reshape(-1)
    pick = (target[None, :] == jnp.arange(BALANCED_TOKENS, dtype=jnp.int32)[:, None]).astype(bf16)
    placed = jnp.dot(
        pick, arrived.reshape(owners * 8, width), preferred_element_type=jnp.float32
    ).astype(bf16)
    all_kv, qd = gather(
        placed, jnp.concatenate([by_head(queries), by_head(output_gradient)], axis=-1)
    )
    all_kv = all_kv.reshape(owners, BALANCED_TOKENS, width)
    qd = qd.reshape(capacity, 2 * GROUP * HEAD_SIZE)

    slot = jnp.arange(capacity, dtype=jnp.int32)
    per_row = extra[:, : 2 * GROUP, :home_rows].transpose(1, 0, 2).reshape(2 * GROUP, capacity)
    per_row = jnp.where(slot[None, :] < count, per_row, 0.0)
    per_row = per_row.reshape(2, GROUP, capacity // ROWS, ROWS).transpose(0, 2, 1, 3)
    per_row = per_row.reshape(2, capacity // ROWS, GROUP * ROWS)
    dq, dkv = attention(
        jnp.stack([first_rank, count]), qd, per_row[0] * LOG2E, per_row[1], all_kv
    )

    summed, dq = reduce(
        dkv.reshape(2, 8, 4, BALANCED_TOKENS, width),
        dq.reshape(heads, home_rows, GROUP * HEAD_SIZE),
    )
    back = lax.dot_general(
        pick, summed, (((0,), (0,)), ((), ())), preferred_element_type=jnp.float32
    ).astype(bf16)
    back = exchange(back.reshape(owners, 8, width), "seq")
    back = lax.dynamic_slice_in_dim(jnp.concatenate([back, back], axis=0), turn, owners, 0)
    back = back[:, :slots].transpose(1, 0, 2).reshape(heads, home_rows, width)
    back = exchange(back, "head")
    query_grads = dq.transpose(1, 0, 2).reshape(home_rows, -1)
    key_grads = back[:, :, :HEAD_SIZE].transpose(1, 0, 2).reshape(home_rows, -1)
    value_grads = back[:, :, HEAD_SIZE:].transpose(1, 0, 2).reshape(home_rows, -1)
    return (query_grads, key_grads, value_grads)


def solution(mesh):
    placed = P(("seq", "head"), None)
    return jax.shard_map(
        per_device,
        mesh=mesh,
        in_specs=(placed,) * 6 + (P(("seq", "head")),),
        out_specs=(placed,) * 3,
        check_vma=False,
    )
```

```python
import jax
import jax.numpy as jnp
from jax import lax
from jax.experimental import pallas as pl
from jax.experimental.pallas import tpu as pltpu
from jax.sharding import PartitionSpec as P

QUERY_HEADS = 40
KEY_VALUE_HEADS = 8
HEAD_SIZE = 128
BALANCED_TOKENS = 128
GROUP = QUERY_HEADS // KEY_VALUE_HEADS
LOG2E = 1.4426950408889634
ROWS = 128
BAND = 16
OWNERS = 16


def attention_kernel(
    meta_ref, qd_ref, lse_ref, delta_ref, kv_ref, dq_ref, dkv_ref, q_sc, g_sc, dq_sc, acc
):
    first = meta_ref[0]
    count = meta_ref[1]
    owners = kv_ref.shape[0]
    blocks = q_sc.shape[0]
    stacked = GROUP * ROWS
    chunk = OWNERS * BAND
    scale = HEAD_SIZE ** (-0.5)
    row_span = BAND * owners
    acc[...] = jnp.zeros_like(acc)
    dq_sc[...] = jnp.zeros_like(dq_sc)
    for b in range(blocks):
        live = (lax.broadcasted_iota(jnp.int32, (ROWS, HEAD_SIZE), 0) + b * ROWS) < count
        for m in range(GROUP):
            rows = pl.ds(b * ROWS, ROWS)
            q = qd_ref[rows, pl.ds(m * HEAD_SIZE, HEAD_SIZE)]
            g = qd_ref[rows, pl.ds((GROUP + m) * HEAD_SIZE, HEAD_SIZE)]
            zero = jnp.zeros((), jnp.float32)
            q_sc[b, pl.ds(m * ROWS, ROWS), :] = jnp.where(
                live, q.astype(jnp.float32), zero
            ).astype(jnp.bfloat16)
            g_sc[b, pl.ds(m * ROWS, ROWS), :] = jnp.where(
                live, g.astype(jnp.float32), zero
            ).astype(jnp.bfloat16)
    live_blocks = (count + ROWS - 1) // ROWS
    key_blocks = (first + count + row_span - 1) // row_span
    index = lax.broadcasted_iota(jnp.int32, (chunk, stacked), 0)
    place_in = index // BAND
    key_local = (index % BAND) * owners + (place_in // 4) * 8 + (place_in % 4) * 2
    row_local = lax.broadcasted_iota(jnp.int32, (chunk, stacked), 1) % ROWS
    gap = key_local - row_local

    def key_block(j, carry):
        lowest = jnp.maximum(j * row_span - first, 0) // ROWS
        band = pl.ds(pl.multiple_of(j * BAND, BAND), BAND)
        for c in range(owners // OWNERS):
            own = pl.ds(c * OWNERS, OWNERS)
            key = kv_ref[own, band, pl.ds(0, HEAD_SIZE)].reshape(chunk, HEAD_SIZE)
            value = kv_ref[own, band, pl.ds(HEAD_SIZE, HEAD_SIZE)].reshape(chunk, HEAD_SIZE)
            key_t = key.astype(jnp.float32).T.astype(jnp.bfloat16)

            def row_block(b, inner):
                q = q_sc[b]
                g = g_sc[b]
                nt = (((1,), (1,)), ((), ()))
                nn = (((1,), (0,)), ((), ()))
                f32 = jnp.float32
                score = lax.dot_general(key, q, nt, preferred_element_type=f32)
                dprob = lax.dot_general(value, g, nt, preferred_element_type=f32)
                limit = first + b * ROWS - j * row_span - (c % 2) * 32 - c // 2
                prob = jnp.where(
                    gap <= limit,
                    jnp.exp2(score * (scale * LOG2E) - lse_ref[pl.ds(b, 1), :]),
                    0.0,
                )
                dscore = prob * (dprob - delta_ref[pl.ds(b, 1), :])
                prob_low = prob.astype(jnp.bfloat16)
                dscore_low = dscore.astype(jnp.bfloat16)
                dk = lax.dot_general(dscore_low, q, nn, preferred_element_type=f32)
                dv = lax.dot_general(prob_low, g, nn, preferred_element_type=f32)
                acc[own, band, pl.ds(0, HEAD_SIZE)] += dk.reshape(OWNERS, BAND, HEAD_SIZE)
                acc[own, band, pl.ds(HEAD_SIZE, HEAD_SIZE)] += dv.reshape(OWNERS, BAND, HEAD_SIZE)
                dq_sc[b] += lax.dot_general(key_t, dscore_low, nn, preferred_element_type=f32)
                return inner

            lax.fori_loop(lowest, live_blocks, row_block, 0)
        return carry

    lax.fori_loop(0, key_blocks, key_block, 0)
    for b in range(blocks):
        for m in range(GROUP):
            part = dq_sc[b, :, pl.ds(m * ROWS, ROWS)].T * scale
            dq_ref[pl.ds(b * ROWS, ROWS), pl.ds(m * HEAD_SIZE, HEAD_SIZE)] = part.astype(
                dq_ref.dtype
            )
    dkv_ref[:, :, pl.ds(0, HEAD_SIZE)] = (acc[:, :, pl.ds(0, HEAD_SIZE)] * scale).astype(
        dkv_ref.dtype
    )
    dkv_ref[:, :, pl.ds(HEAD_SIZE, HEAD_SIZE)] = acc[:, :, pl.ds(HEAD_SIZE, HEAD_SIZE)].astype(
        dkv_ref.dtype
    )


def attention(meta, qd, lse, delta, kv, interpret=False):
    capacity = qd.shape[0]
    owners, per_owner, width = kv.shape
    blocks = capacity // ROWS
    vmem = pl.BlockSpec(memory_space=pltpu.VMEM)
    return pl.pallas_call(
        attention_kernel,
        name="attention",
        out_shape=(
            jax.ShapeDtypeStruct((capacity, GROUP * HEAD_SIZE), jnp.bfloat16),
            jax.ShapeDtypeStruct(kv.shape, jnp.bfloat16),
        ),
        in_specs=[pl.BlockSpec(memory_space=pltpu.SMEM), vmem, vmem, vmem, vmem],
        out_specs=(vmem, vmem),
        scratch_shapes=[
            pltpu.VMEM((blocks, GROUP * ROWS, HEAD_SIZE), jnp.bfloat16),
            pltpu.VMEM((blocks, GROUP * ROWS, HEAD_SIZE), jnp.bfloat16),
            pltpu.VMEM((blocks, HEAD_SIZE, GROUP * ROWS), jnp.float32),
            pltpu.VMEM(kv.shape, jnp.float32),
        ],
        compiler_params=pltpu.CompilerParams(vmem_limit_bytes=56 << 20),
        cost_estimate=pl.CostEstimate(
            flops=10 * capacity * GROUP * HEAD_SIZE * owners * per_owner // 2,
            bytes_accessed=2 * (2 * kv.size + 3 * qd.size),
            transcendentals=0,
        ),
        interpret=interpret,
    )(meta, qd, lse, delta, kv)


def place(seq_index):
    return seq_index // 8, (seq_index // 2) % 4, seq_index % 2


def peers():
    seq = lax.axis_index("seq")
    head = lax.axis_index("head")
    z, x, core = place(seq)
    spot = lambda z, x, core: (z * 8 + x * 2 + core, head)
    to_z = [None] + [spot((z + d) % 8, x, core) for d in range(1, 8)]
    to_x = [None] + [spot(z, (x + e) % 4, core) for e in range(1, 4)]
    partner = spot(z, x, 1 - core)
    to_head = [None] + [(seq, (head + d) % 8) for d in range(1, 8)]
    return z, x, core, head, to_z, to_x, partner, to_head


def meet(groups):
    barrier = pltpu.get_barrier_semaphore()
    seq = lax.axis_index("seq")
    head = lax.axis_index("head")

    def greet(k, carry):
        pl.semaphore_signal(
            barrier,
            inc=1,
            device_id=((seq + k) % 64, head),
            device_id_type=pl.DeviceIdType.MESH,
        )
        return carry

    lax.fori_loop(1, 64, greet, 0)
    total = 63
    for group in groups:
        for device in group:
            pl.semaphore_signal(
                barrier, inc=1, device_id=device, device_id_type=pl.DeviceIdType.MESH
            )
            total += 1
    pl.semaphore_wait(barrier, total)


def remote(src, dst, send, recv, device):
    return pltpu.make_async_remote_copy(
        src_ref=src,
        dst_ref=dst,
        send_sem=send,
        recv_sem=recv,
        device_id=device,
        device_id_type=pl.DeviceIdType.MESH,
    )


def scatter_seq(out_ref, in_ref, own_sem, send, recv):
    seq = lax.axis_index("seq")
    head = lax.axis_index("head")
    own = pltpu.make_async_copy(out_ref.at[seq], in_ref.at[seq], own_sem)
    own.start()

    def copy(k):
        there = (seq + k) % 64
        return remote(
            out_ref.at[there], in_ref.at[seq], send.at[k], recv.at[k], (there, head)
        )

    def start(k, carry):
        copy(k).start()
        return carry

    def finish(k, carry):
        from_there = in_ref.at[(seq + 64 - k) % 64]
        arrived = remote(
            from_there, from_there, send.at[k], recv.at[k], ((seq + k) % 64, head)
        )
        arrived.wait_recv()
        return carry

    def sent(k, carry):
        copy(k).wait_send()
        return carry

    lax.fori_loop(1, 64, start, 0)
    lax.fori_loop(1, 64, finish, 0)
    own.wait()
    return lambda: lax.fori_loop(1, 64, sent, 0)


def scatter_head(out_ref, in_ref, head, own_sem, send, recv, to_head):
    copies = []
    for d in NEAR_FIRST[1:]:
        copy = remote(
            out_ref.at[(head + d) % 8], in_ref.at[head], send.at[d], recv.at[d], to_head[d]
        )
        copy.start()
        copies.append(copy)
    own = pltpu.make_async_copy(out_ref.at[head], in_ref.at[head], own_sem)
    own.start()

    def finish():
        for d in NEAR_FIRST[1:]:
            part = in_ref.at[(head + 8 - d) % 8]
            remote(part, part, send.at[d], recv.at[d], to_head[d]).wait_recv()
        own.wait()

    return copies, finish


def wide(value, shape):
    return jnp.broadcast_to(value, shape)


NEAR_FIRST = (0, 1, 7, 2, 6, 3, 5, 4)


def gather_kernel(
    pack_ref, qd_ref, kv_ref, rows_ref, got_ref, pick_ref, to_owner, at_owner, own_ref, own_sem,
    z_send, z_recv, x_send, x_recv, p_send, p_recv, h_send, h_recv, k_send, k_recv, s_send, s_recv,
):
    z, x, core, head, to_z, to_x, partner, to_head = peers()
    f32 = jnp.float32
    i32 = jnp.int32
    bf16 = jnp.bfloat16
    meet((to_head[1:],))
    copies, arrive = scatter_head(
        pack_ref, got_ref, head, own_sem.at[0], k_send, k_recv, to_head
    )
    arrive()
    more, arrive_rows = scatter_head(
        qd_ref, rows_ref, head, own_sem.at[1], h_send, h_recv, to_head
    )
    copies = copies + more
    home = got_ref.shape[1] - 16
    capacity = 8 * home
    slots = capacity // 64
    notes = got_ref[0, pl.ds(home, 16), :].astype(f32)
    first = (notes[10:11, 0:1] * 128 + notes[10:11, 1:2]).astype(i32)
    count = notes[10:11, 2:3]
    for h in range(1, 8):
        count = count + got_ref[h, pl.ds(home, 16), :].astype(f32)[10:11, 2:3]
    count = count.astype(i32)
    shape = (1024, capacity)
    row = lax.broadcasted_iota(i32, shape, 0)
    column = lax.broadcasted_iota(i32, shape, 1)
    wanted = (row % 8) * 64 + ((row // 16 - wide(first, shape)) & 63)
    hit = (column == wanted) & (row % 8 < slots)
    is_key = (row // 8) % 2 == 0
    one = jnp.ones((), f32)
    zero = jnp.zeros((), f32)
    take_key = jnp.where(hit & is_key, one, zero).astype(bf16)
    take_value = jnp.where(hit & ~is_key, one, zero).astype(bf16)
    pairs = got_ref[:, pl.ds(0, home), :].reshape(capacity, 2 * HEAD_SIZE)
    sent = jnp.dot(take_key, pairs[:, :HEAD_SIZE], preferred_element_type=f32) + jnp.dot(
        take_value, pairs[:, HEAD_SIZE:], preferred_element_type=f32
    )
    shape = (1024, HEAD_SIZE)
    row = lax.broadcasted_iota(i32, shape, 0)
    lane = lax.broadcasted_iota(i32, shape, 1)
    first_wide = wide(first, shape)
    count_wide = wide(count, shape)
    note = jnp.where(
        lane == 0,
        first_wide >> 7,
        jnp.where(
            lane == 1,
            first_wide & 127,
            jnp.where(lane == 2, count_wide >> 7, jnp.where(lane == 3, count_wide & 127, 0)),
        ),
    ).astype(f32)
    sent = jnp.where(row % 16 == slots, note, sent)
    to_owner[...] = sent.astype(bf16).reshape(64, 16, HEAD_SIZE)
    drain = scatter_seq(to_owner, at_owner, own_sem.at[2], s_send, s_recv)
    come = at_owner[...].reshape(1024, HEAD_SIZE)
    told = come.astype(f32).reshape(64, 16, HEAD_SIZE)[:, slots : slots + 1, :]
    told = wide(told, (64, 16, HEAD_SIZE)).reshape(1024, HEAD_SIZE)
    starts = wide((told[:, 0:1] * 128 + told[:, 1:2]).astype(i32), shape)
    counts = wide((told[:, 2:3] * 128 + told[:, 3:4]).astype(i32), shape)
    turn = row % 8
    within = turn * 64 + ((lax.axis_index("seq") - starts) & 63)
    alive = (within < counts) & (turn < slots)
    target = jnp.where(alive, (starts + within) >> 6, -1)
    pick = jnp.where(target == lane, one, zero)
    pick_ref[...] = pick.astype(bf16)
    is_key = (row // 8) % 2 == 0
    for half in range(2):
        chosen = jnp.where(is_key if half == 0 else ~is_key, pick, zero).T.astype(bf16)
        own_ref[:, pl.ds(half * HEAD_SIZE, HEAD_SIZE)] = jnp.dot(
            chosen, come, preferred_element_type=f32
        ).astype(bf16)
    for d in NEAR_FIRST[1:]:
        copy = remote(own_ref, kv_ref.at[core, z, x], z_send.at[d], z_recv.at[d], to_z[d])
        copy.start()
        copies.append(copy)
    mine = pltpu.make_async_copy(own_ref, kv_ref.at[core, z, x], own_sem.at[3])
    mine.start()
    for d in NEAR_FIRST:
        source = (z + 8 - d) % 8
        block = kv_ref.at[core, source, x]
        if d == 0:
            mine.wait()
        else:
            remote(own_ref, block, z_send.at[d], z_recv.at[d], to_z[d]).wait_recv()
        for e in (1, 3, 2):
            copy = remote(block, block, x_send.at[d, e], x_recv.at[d, e], to_x[e])
            copy.start()
            copies.append(copy)
    for d in NEAR_FIRST:
        source = (z + 8 - d) % 8
        for e in (1, 3, 2):
            block = kv_ref.at[core, source, (x + 4 - e) % 4]
            remote(block, block, x_send.at[d, e], x_recv.at[d, e], to_x[e]).wait_recv()
        row = kv_ref.at[core, source]
        copy = remote(row, row, p_send.at[d], p_recv.at[d], partner)
        copy.start()
        copies.append(copy)
    for d in NEAR_FIRST:
        row = kv_ref.at[1 - core, (z + 8 - d) % 8]
        remote(row, row, p_send.at[d], p_recv.at[d], partner).wait_recv()
    arrive_rows()
    drain()
    for copy in copies:
        copy.wait_send()


def gather(pack, qd):
    vmem = pl.BlockSpec(memory_space=pltpu.VMEM)
    dma = pltpu.SemaphoreType.DMA
    return pl.pallas_call(
        gather_kernel,
        name="gather",
        out_shape=(
            jax.ShapeDtypeStruct((2, 8, 4, BALANCED_TOKENS, 2 * HEAD_SIZE), pack.dtype),
            jax.ShapeDtypeStruct(qd.shape, qd.dtype),
            jax.ShapeDtypeStruct(pack.shape, pack.dtype),
            jax.ShapeDtypeStruct((1024, BALANCED_TOKENS), pack.dtype),
        ),
        in_specs=[vmem, vmem],
        out_specs=(vmem,) * 4,
        scratch_shapes=[
            pltpu.VMEM((64, 16, HEAD_SIZE), pack.dtype),
            pltpu.VMEM((64, 16, HEAD_SIZE), pack.dtype),
            pltpu.VMEM((BALANCED_TOKENS, 2 * HEAD_SIZE), pack.dtype),
            dma((4,)), dma((8,)), dma((8,)), dma((8, 4)), dma((8, 4)), dma((8,)), dma((8,)),
            dma((8,)), dma((8,)), dma((8,)), dma((8,)), dma((64,)), dma((64,)),
        ],
        compiler_params=pltpu.CompilerParams(
            collective_id=0, has_side_effects=True, vmem_limit_bytes=48 << 20
        ),
    )(pack, qd)


def reduce_kernel(
    first_ref, pick_ref, kv_ref, dq_ref, grad_ref, rows_ref, from_core, to_row, from_row, to_column,
    from_column, total, to_home, at_home, to_slot, own_sem, p_send, p_recv, x_send, x_recv, z_send,
    z_recv, h_send, h_recv, k_send, k_recv, s_send, s_recv,
):
    z, x, core, head, to_z, to_x, partner, to_head = peers()
    f32 = jnp.float32
    meet((to_head[1:],))
    order = (4, 3, 5, 2, 6, 1, 7, 0)
    copies = []
    for d in order:
        there = (z + d) % 8
        copy = remote(
            kv_ref.at[1 - core, there], from_core.at[there], p_send.at[d], p_recv.at[d], partner
        )
        copy.start()
        copies.append(copy)
    more, arrive_rows = scatter_head(
        dq_ref, rows_ref, head, own_sem.at[0], h_send, h_recv, to_head
    )
    copies = copies + more
    for d in order:
        there = (z + d) % 8
        remote(
            kv_ref.at[1 - core, there], from_core.at[there], p_send.at[d], p_recv.at[d], partner
        ).wait_recv()
        for e in (2, 1, 3):
            other = (x + e) % 4
            to_row[e, d] = (
                kv_ref[core, there, other].astype(f32) + from_core[there, other].astype(f32)
            ).astype(to_row.dtype)
            copy = remote(
                to_row.at[e, d], from_row.at[e, d], x_send.at[e, d], x_recv.at[e, d], to_x[e]
            )
            copy.start()
            copies.append(copy)
    for d in order:
        there = (z + d) % 8
        part = kv_ref[core, there, x].astype(f32) + from_core[there, x].astype(f32)
        for e in (1, 3, 2):
            remote(
                to_row.at[e, d], from_row.at[e, d], x_send.at[e, d], x_recv.at[e, d], to_x[e]
            ).wait_recv()
            part = part + from_row[e, d].astype(f32)
        if d == 0:
            total[...] = part
        else:
            to_column[d] = part.astype(to_column.dtype)
            copy = remote(
                to_column.at[d], from_column.at[d], z_send.at[d], z_recv.at[d], to_z[d]
            )
            copy.start()
            copies.append(copy)
    part = total[...]
    for d in order[:-1]:
        remote(
            to_column.at[d], from_column.at[d], z_send.at[d], z_recv.at[d], to_z[d]
        ).wait_recv()
        part = part + from_column[d].astype(f32)
    i32 = jnp.int32
    bf16 = jnp.bfloat16
    one = jnp.ones((), f32)
    zero = jnp.zeros((), f32)
    part = part.astype(bf16)
    pick = pick_ref[...].astype(f32)
    is_key = (lax.broadcasted_iota(i32, pick.shape, 0) // 8) % 2 == 0
    sent = jnp.dot(
        jnp.where(is_key, pick, zero).astype(bf16), part[:, :HEAD_SIZE], preferred_element_type=f32
    ) + jnp.dot(
        jnp.where(is_key, zero, pick).astype(bf16), part[:, HEAD_SIZE:], preferred_element_type=f32
    )
    to_home[...] = sent.astype(bf16).reshape(64, 16, HEAD_SIZE)
    drain = scatter_seq(to_home, at_home, own_sem.at[1], s_send, s_recv)
    home = to_slot.shape[1]
    shape = (8 * home, 1024)
    slot = lax.broadcasted_iota(i32, shape, 0)
    column = lax.broadcasted_iota(i32, shape, 1)
    wanted = (((slot & 63) + wide(first_ref[0:1, 0:1], shape)) & 63) * 16 + (slot >> 6)
    come = at_home[...].reshape(1024, HEAD_SIZE)
    for half in range(2):
        chosen = jnp.where(column == wanted + 8 * half, one, zero).astype(bf16)
        to_slot[:, :, pl.ds(half * HEAD_SIZE, HEAD_SIZE)] = (
            jnp.dot(chosen, come, preferred_element_type=f32)
            .astype(bf16)
            .reshape(8, home, HEAD_SIZE)
        )
    more, arrive = scatter_head(
        to_slot, grad_ref, head, own_sem.at[2], k_send, k_recv, to_head
    )
    copies = copies + more
    arrive_rows()
    arrive()
    drain()
    for copy in copies:
        copy.wait_send()


def reduce(first, pick, dkv, dq):
    vmem = pl.BlockSpec(memory_space=pltpu.VMEM)
    dma = pltpu.SemaphoreType.DMA
    block = dkv.shape[3:]
    bf16 = jnp.bfloat16
    return pl.pallas_call(
        reduce_kernel,
        name="reduce",
        out_shape=(
            jax.ShapeDtypeStruct(dq.shape[:2] + (2 * HEAD_SIZE,), bf16),
            jax.ShapeDtypeStruct(dq.shape, dq.dtype),
        ),
        in_specs=[vmem] * 4,
        out_specs=(vmem, vmem),
        scratch_shapes=[
            pltpu.VMEM((8, 4) + block, bf16),
            pltpu.VMEM((4, 8) + block, bf16),
            pltpu.VMEM((4, 8) + block, bf16),
            pltpu.VMEM((8,) + block, bf16),
            pltpu.VMEM((8,) + block, bf16),
            pltpu.VMEM(block, jnp.float32),
            pltpu.VMEM((64, 16, HEAD_SIZE), bf16),
            pltpu.VMEM((64, 16, HEAD_SIZE), bf16),
            pltpu.VMEM(dq.shape[:2] + (2 * HEAD_SIZE,), bf16),
            dma((3,)), dma((8,)), dma((8,)), dma((4, 8)), dma((4, 8)), dma((8,)), dma((8,)),
            dma((8,)), dma((8,)), dma((8,)), dma((8,)), dma((64,)), dma((64,)),
        ],
        compiler_params=pltpu.CompilerParams(
            collective_id=1, has_side_effects=True, vmem_limit_bytes=40 << 20
        ),
    )(first, pick, dkv, dq)


def per_device(queries, keys, values, outputs, output_gradient, lse, ranks):
    owners = lax.axis_size("seq")
    heads = lax.axis_size("head")
    home_rows = queries.shape[0]
    capacity = home_rows * heads
    survivors = BALANCED_TOKENS * owners
    bf16 = jnp.bfloat16
    width = 2 * HEAD_SIZE

    dots = jnp.sum(
        output_gradient.astype(jnp.float32).reshape(home_rows, QUERY_HEADS, HEAD_SIZE)
        * outputs.astype(jnp.float32).reshape(home_rows, QUERY_HEADS, HEAD_SIZE),
        axis=-1,
    ).astype(bf16)

    def by_head(array):
        return array.reshape(home_rows, heads, -1).transpose(1, 0, 2)

    living = jnp.sum((ranks < survivors).astype(jnp.int32))
    digits = jnp.stack([ranks[0] // 128, ranks[0] % 128, living]).astype(bf16)
    small = jnp.concatenate([by_head(lse), by_head(dots)], axis=-1).transpose(0, 2, 1)
    small = jnp.pad(small, ((0, 0), (0, 0), (0, width - home_rows)))
    digit_rows = jnp.broadcast_to(
        jnp.pad(digits, (0, width - 3))[None, None], (heads, 16 - 2 * GROUP, width)
    )
    first_pack = jnp.concatenate(
        [jnp.concatenate([by_head(keys), by_head(values)], axis=-1), small, digit_rows], axis=1
    )
    all_kv, qd, first_pack, pick = gather(
        first_pack, jnp.concatenate([by_head(queries), by_head(output_gradient)], axis=-1)
    )
    extra = first_pack[:, home_rows:].astype(jnp.float32)
    first_rank = (extra[0, 2 * GROUP, 0] * 128 + extra[0, 2 * GROUP, 1]).astype(jnp.int32)
    count = jnp.sum(extra[:, 2 * GROUP, 2]).astype(jnp.int32)

    all_kv = all_kv.reshape(owners, BALANCED_TOKENS, width)
    qd = qd.reshape(capacity, 2 * GROUP * HEAD_SIZE)

    slot = jnp.arange(capacity, dtype=jnp.int32)
    per_row = extra[:, : 2 * GROUP, :home_rows].transpose(1, 0, 2).reshape(2 * GROUP, capacity)
    per_row = jnp.where(slot[None, :] < count, per_row, 0.0)
    per_row = per_row.reshape(2, GROUP, capacity // ROWS, ROWS).transpose(0, 2, 1, 3)
    per_row = per_row.reshape(2, capacity // ROWS, GROUP * ROWS)
    dq, dkv = attention(
        jnp.stack([first_rank, count]), qd, per_row[0] * LOG2E, per_row[1], all_kv
    )

    back, dq = reduce(
        jnp.broadcast_to(first_rank, (8, HEAD_SIZE)),
        pick,
        dkv.reshape(2, 8, 4, BALANCED_TOKENS, width),
        dq.reshape(heads, home_rows, GROUP * HEAD_SIZE),
    )
    query_grads = dq.transpose(1, 0, 2).reshape(home_rows, -1)
    key_grads = back[:, :, :HEAD_SIZE].transpose(1, 0, 2).reshape(home_rows, -1)
    value_grads = back[:, :, HEAD_SIZE:].transpose(1, 0, 2).reshape(home_rows, -1)
    return (query_grads, key_grads, value_grads)


def solution(mesh):
    placed = P(("seq", "head"), None)
    return jax.shard_map(
        per_device,
        mesh=mesh,
        in_specs=(placed,) * 6 + (P(("seq", "head")),),
        out_specs=(placed,) * 3,
        check_vma=False,
    )
```

```python
import jax
import jax.numpy as jnp
from jax import lax
from jax.experimental import pallas as pl
from jax.experimental.pallas import tpu as pltpu
from jax.sharding import PartitionSpec as P

QUERY_HEADS = 40
KEY_VALUE_HEADS = 8
HEAD_SIZE = 128
BALANCED_TOKENS = 128
GROUP = QUERY_HEADS // KEY_VALUE_HEADS
LOG2E = 1.4426950408889634
ROWS = 128
BAND = 16
OWNERS = 16


def attention_kernel(
    meta_ref, qd_ref, stat_ref, kv_ref, dq_ref, dkv_ref, q_sc, g_sc, dq_sc, acc
):
    first = meta_ref[0, 0]
    count = meta_ref[0, 1]
    owners = kv_ref.shape[0]
    blocks = q_sc.shape[0]
    stacked = GROUP * ROWS
    chunk = OWNERS * BAND
    scale = HEAD_SIZE ** (-0.5)
    row_span = BAND * owners
    acc[...] = jnp.zeros_like(acc)
    dq_sc[...] = jnp.zeros_like(dq_sc)
    for b in range(blocks):
        live = (lax.broadcasted_iota(jnp.int32, (ROWS, HEAD_SIZE), 0) + b * ROWS) < count
        for m in range(GROUP):
            rows = pl.ds(b * ROWS, ROWS)
            q = qd_ref[rows, pl.ds(m * HEAD_SIZE, HEAD_SIZE)]
            g = qd_ref[rows, pl.ds((GROUP + m) * HEAD_SIZE, HEAD_SIZE)]
            zero = jnp.zeros((), jnp.float32)
            q_sc[b, pl.ds(m * ROWS, ROWS), :] = jnp.where(
                live, q.astype(jnp.float32), zero
            ).astype(jnp.bfloat16)
            g_sc[b, pl.ds(m * ROWS, ROWS), :] = jnp.where(
                live, g.astype(jnp.float32), zero
            ).astype(jnp.bfloat16)
    live_blocks = (count + ROWS - 1) // ROWS
    key_blocks = (first + count + row_span - 1) // row_span
    index = lax.broadcasted_iota(jnp.int32, (chunk, stacked), 0)
    place_in = index // BAND
    key_local = (index % BAND) * owners + (place_in // 4) * 8 + (place_in % 4) * 2
    row_local = lax.broadcasted_iota(jnp.int32, (chunk, stacked), 1) % ROWS
    gap = key_local - row_local

    def key_block(j, carry):
        lowest = jnp.maximum(j * row_span - first, 0) // ROWS
        band = pl.ds(pl.multiple_of(j * BAND, BAND), BAND)
        for c in range(owners // OWNERS):
            own = pl.ds(c * OWNERS, OWNERS)
            key = kv_ref[own, band, pl.ds(0, HEAD_SIZE)].reshape(chunk, HEAD_SIZE)
            value = kv_ref[own, band, pl.ds(HEAD_SIZE, HEAD_SIZE)].reshape(chunk, HEAD_SIZE)
            key_t = key.astype(jnp.float32).T.astype(jnp.bfloat16)

            def row_block(b, inner):
                q = q_sc[b]
                g = g_sc[b]
                nt = (((1,), (1,)), ((), ()))
                nn = (((1,), (0,)), ((), ()))
                f32 = jnp.float32
                score = lax.dot_general(key, q, nt, preferred_element_type=f32)
                dprob = lax.dot_general(value, g, nt, preferred_element_type=f32)
                limit = first + b * ROWS - j * row_span - (c % 2) * 32 - c // 2
                prob = jnp.where(
                    gap <= limit,
                    jnp.exp2(score * (scale * LOG2E) - stat_ref[0, pl.ds(b, 1), :]),
                    0.0,
                )
                dscore = prob * (dprob - stat_ref[1, pl.ds(b, 1), :])
                prob_low = prob.astype(jnp.bfloat16)
                dscore_low = dscore.astype(jnp.bfloat16)
                dk = lax.dot_general(dscore_low, q, nn, preferred_element_type=f32)
                dv = lax.dot_general(prob_low, g, nn, preferred_element_type=f32)
                acc[own, band, pl.ds(0, HEAD_SIZE)] += dk.reshape(OWNERS, BAND, HEAD_SIZE)
                acc[own, band, pl.ds(HEAD_SIZE, HEAD_SIZE)] += dv.reshape(OWNERS, BAND, HEAD_SIZE)
                dq_sc[b] += lax.dot_general(key_t, dscore_low, nn, preferred_element_type=f32)
                return inner

            lax.fori_loop(lowest, live_blocks, row_block, 0)
        return carry

    lax.fori_loop(0, key_blocks, key_block, 0)
    for b in range(blocks):
        for m in range(GROUP):
            part = dq_sc[b, :, pl.ds(m * ROWS, ROWS)].T * scale
            dq_ref[pl.ds(b * ROWS, ROWS), pl.ds(m * HEAD_SIZE, HEAD_SIZE)] = part.astype(
                dq_ref.dtype
            )
    dkv_ref[:, :, pl.ds(0, HEAD_SIZE)] = (acc[:, :, pl.ds(0, HEAD_SIZE)] * scale).astype(
        dkv_ref.dtype
    )
    dkv_ref[:, :, pl.ds(HEAD_SIZE, HEAD_SIZE)] = acc[:, :, pl.ds(HEAD_SIZE, HEAD_SIZE)].astype(
        dkv_ref.dtype
    )


def attention(meta, qd, stats, kv, interpret=False):
    capacity = qd.shape[0]
    owners, per_owner, width = kv.shape
    blocks = capacity // ROWS
    vmem = pl.BlockSpec(memory_space=pltpu.VMEM)
    return pl.pallas_call(
        attention_kernel,
        name="attention",
        out_shape=(
            jax.ShapeDtypeStruct((capacity, GROUP * HEAD_SIZE), jnp.bfloat16),
            jax.ShapeDtypeStruct(kv.shape, jnp.bfloat16),
        ),
        in_specs=[pl.BlockSpec(memory_space=pltpu.SMEM), vmem, vmem, vmem],
        out_specs=(vmem, vmem),
        scratch_shapes=[
            pltpu.VMEM((blocks, GROUP * ROWS, HEAD_SIZE), jnp.bfloat16),
            pltpu.VMEM((blocks, GROUP * ROWS, HEAD_SIZE), jnp.bfloat16),
            pltpu.VMEM((blocks, HEAD_SIZE, GROUP * ROWS), jnp.float32),
            pltpu.VMEM(kv.shape, jnp.float32),
        ],
        compiler_params=pltpu.CompilerParams(vmem_limit_bytes=26 << 20),
        cost_estimate=pl.CostEstimate(
            flops=10 * capacity * GROUP * HEAD_SIZE * owners * per_owner // 2,
            bytes_accessed=2 * (2 * kv.size + 3 * qd.size),
            transcendentals=0,
        ),
        interpret=interpret,
    )(meta, qd, stats, kv)


def place(seq_index):
    return seq_index // 8, (seq_index // 2) % 4, seq_index % 2


def peers():
    seq = lax.axis_index("seq")
    head = lax.axis_index("head")
    z, x, core = place(seq)
    spot = lambda z, x, core: (z * 8 + x * 2 + core, head)
    to_z = [None] + [spot((z + d) % 8, x, core) for d in range(1, 8)]
    to_x = [None] + [spot(z, (x + e) % 4, core) for e in range(1, 4)]
    partner = spot(z, x, 1 - core)
    to_head = [None] + [(seq, (head + d) % 8) for d in range(1, 8)]
    return z, x, core, head, to_z, to_x, partner, to_head


def meet(groups):
    barrier = pltpu.get_barrier_semaphore()
    seq = lax.axis_index("seq")
    head = lax.axis_index("head")

    def greet(k, carry):
        pl.semaphore_signal(
            barrier,
            inc=1,
            device_id=((seq + k) % 64, head),
            device_id_type=pl.DeviceIdType.MESH,
        )
        return carry

    lax.fori_loop(1, 64, greet, 0)
    total = 63
    for group in groups:
        for device in group:
            pl.semaphore_signal(
                barrier, inc=1, device_id=device, device_id_type=pl.DeviceIdType.MESH
            )
            total += 1
    pl.semaphore_wait(barrier, total)


def remote(src, dst, send, recv, device):
    return pltpu.make_async_remote_copy(
        src_ref=src,
        dst_ref=dst,
        send_sem=send,
        recv_sem=recv,
        device_id=device,
        device_id_type=pl.DeviceIdType.MESH,
    )


def scatter_seq(out_ref, in_ref, own_sem, send, recv):
    seq = lax.axis_index("seq")
    head = lax.axis_index("head")
    own = pltpu.make_async_copy(out_ref.at[seq], in_ref.at[seq], own_sem)
    own.start()

    def copy(k):
        there = (seq + k) % 64
        return remote(
            out_ref.at[there], in_ref.at[seq], send.at[k], recv.at[k], (there, head)
        )

    def start(k, carry):
        copy(k).start()
        return carry

    def finish(k, carry):
        from_there = in_ref.at[(seq + 64 - k) % 64]
        arrived = remote(
            from_there, from_there, send.at[k], recv.at[k], ((seq + k) % 64, head)
        )
        arrived.wait_recv()
        return carry

    def sent(k, carry):
        copy(k).wait_send()
        return carry

    def lands():
        lax.fori_loop(1, 64, finish, 0)
        own.wait()

    lax.fori_loop(1, 64, start, 0)
    return lands, lambda: lax.fori_loop(1, 64, sent, 0)


def scatter_head(out_ref, in_ref, head, own_sem, send, recv, to_head):
    copies = []
    for d in NEAR_FIRST[1:]:
        copy = remote(
            out_ref.at[(head + d) % 8], in_ref.at[head], send.at[d], recv.at[d], to_head[d]
        )
        copy.start()
        copies.append(copy)
    own = pltpu.make_async_copy(out_ref.at[head], in_ref.at[head], own_sem)
    own.start()

    def finish():
        for d in NEAR_FIRST[1:]:
            part = in_ref.at[(head + 8 - d) % 8]
            remote(part, part, send.at[d], recv.at[d], to_head[d]).wait_recv()
        own.wait()

    return copies, finish


def wide(value, shape):
    return jnp.broadcast_to(value, shape)


NEAR_FIRST = (0, 1, 7, 2, 6, 3, 5, 4)


def gather_kernel(
    pack_ref, qd_ref, kv_ref, rows_ref, meta_ref, stat_ref, pick_ref, got_ref, to_owner, at_owner,
    own_ref, own_sem,
    z_send, z_recv, x_send, x_recv, p_send, p_recv, h_send, h_recv, k_send, k_recv, s_send, s_recv,
):
    z, x, core, head, to_z, to_x, partner, to_head = peers()
    f32 = jnp.float32
    i32 = jnp.int32
    bf16 = jnp.bfloat16
    meet((to_head[1:],))
    copies, arrive = scatter_head(
        pack_ref, got_ref, head, own_sem.at[0], k_send, k_recv, to_head
    )
    arrive()
    more, arrive_rows = scatter_head(
        qd_ref, rows_ref, head, own_sem.at[1], h_send, h_recv, to_head
    )
    copies = copies + more
    home = got_ref.shape[1] - 16
    capacity = 8 * home
    slots = capacity // 64
    notes = got_ref[0, pl.ds(home, 16), :].astype(f32)
    first = (notes[10:11, 0:1] * 128 + notes[10:11, 1:2]).astype(i32)
    count = notes[10:11, 2:3]
    for h in range(1, 8):
        count = count + got_ref[h, pl.ds(home, 16), :].astype(f32)[10:11, 2:3]
    count = count.astype(i32)
    shape = (1024, capacity)
    row = lax.broadcasted_iota(i32, shape, 0)
    column = lax.broadcasted_iota(i32, shape, 1)
    wanted = (row % 8) * 64 + ((row // 16 - wide(first, shape)) & 63)
    hit = (column == wanted) & (row % 8 < slots)
    is_key = (row // 8) % 2 == 0
    one = jnp.ones((), f32)
    zero = jnp.zeros((), f32)
    take_key = jnp.where(hit & is_key, one, zero).astype(bf16)
    take_value = jnp.where(hit & ~is_key, one, zero).astype(bf16)
    pairs = got_ref[:, pl.ds(0, home), :].reshape(capacity, 2 * HEAD_SIZE)
    sent = jnp.dot(take_key, pairs[:, :HEAD_SIZE], preferred_element_type=f32) + jnp.dot(
        take_value, pairs[:, HEAD_SIZE:], preferred_element_type=f32
    )
    shape = (1024, HEAD_SIZE)
    row = lax.broadcasted_iota(i32, shape, 0)
    lane = lax.broadcasted_iota(i32, shape, 1)
    first_wide = wide(first, shape)
    count_wide = wide(count, shape)
    note = jnp.where(
        lane == 0,
        first_wide >> 7,
        jnp.where(
            lane == 1,
            first_wide & 127,
            jnp.where(lane == 2, count_wide >> 7, jnp.where(lane == 3, count_wide & 127, 0)),
        ),
    ).astype(f32)
    sent = jnp.where(row % 16 == slots, note, sent)
    to_owner[...] = sent.astype(bf16).reshape(64, 16, HEAD_SIZE)
    lands, drain = scatter_seq(to_owner, at_owner, own_sem.at[2], s_send, s_recv)
    shape = meta_ref.shape
    lane_of = lax.broadcasted_iota(i32, shape, 1)
    meta_ref[...] = jnp.where(
        lane_of == 0, wide(first, shape), jnp.where(lane_of == 1, wide(count, shape), 0)
    )
    shape = (2 * HEAD_SIZE, capacity)
    apart = lax.broadcasted_iota(i32, shape, 1) - lax.broadcasted_iota(i32, shape, 0)
    inside = lax.broadcasted_iota(i32, shape, 0) < home
    stats = jnp.zeros((16, capacity), f32)
    for h in range(8):
        spread = jnp.where(inside & (apart == h * home), one, zero).astype(bf16)
        stats = stats + jnp.dot(
            got_ref[h, pl.ds(home, 16), :], spread, preferred_element_type=f32
        )
    slot = lax.broadcasted_iota(i32, stats.shape, 1)
    stats = jnp.where(slot < wide(count, stats.shape), stats, 0.0)
    for b in range(capacity // ROWS):
        for m in range(GROUP):
            lanes = pl.ds(m * ROWS, ROWS)
            part = stats[:, b * ROWS : (b + 1) * ROWS]
            stat_ref[0, pl.ds(b, 1), lanes] = part[m : m + 1] * LOG2E
            stat_ref[1, pl.ds(b, 1), lanes] = part[GROUP + m : GROUP + m + 1]
    shape = (1024, HEAD_SIZE)
    lands()
    come = at_owner[...].reshape(1024, HEAD_SIZE)
    told = come.astype(f32).reshape(64, 16, HEAD_SIZE)[:, slots : slots + 1, :]
    told = wide(told, (64, 16, HEAD_SIZE)).reshape(1024, HEAD_SIZE)
    starts = wide((told[:, 0:1] * 128 + told[:, 1:2]).astype(i32), shape)
    counts = wide((told[:, 2:3] * 128 + told[:, 3:4]).astype(i32), shape)
    turn = row % 8
    within = turn * 64 + ((lax.axis_index("seq") - starts) & 63)
    alive = (within < counts) & (turn < slots)
    target = jnp.where(alive, (starts + within) >> 6, -1)
    pick = jnp.where(target == lane, one, zero)
    pick_ref[...] = pick.astype(bf16)
    is_key = (row // 8) % 2 == 0
    for half in range(2):
        chosen = jnp.where(is_key if half == 0 else ~is_key, pick, zero).T.astype(bf16)
        own_ref[:, pl.ds(half * HEAD_SIZE, HEAD_SIZE)] = jnp.dot(
            chosen, come, preferred_element_type=f32
        ).astype(bf16)
    for d in NEAR_FIRST[1:]:
        copy = remote(own_ref, kv_ref.at[core, z, x], z_send.at[d], z_recv.at[d], to_z[d])
        copy.start()
        copies.append(copy)
    mine = pltpu.make_async_copy(own_ref, kv_ref.at[core, z, x], own_sem.at[3])
    mine.start()
    for d in NEAR_FIRST:
        source = (z + 8 - d) % 8
        block = kv_ref.at[core, source, x]
        if d == 0:
            mine.wait()
        else:
            remote(own_ref, block, z_send.at[d], z_recv.at[d], to_z[d]).wait_recv()
        for e in (1, 3):
            copy = remote(block, block, x_send.at[d, e], x_recv.at[d, e], to_x[e])
            copy.start()
            copies.append(copy)
    half = BALANCED_TOKENS // 2
    for d in NEAR_FIRST:
        source = (z + 8 - d) % 8
        for e, onward in ((1, 0), (3, 2)):
            block = kv_ref.at[core, source, (x + 4 - e) % 4]
            remote(block, block, x_send.at[d, e], x_recv.at[d, e], to_x[e]).wait_recv()
            part = block.at[pl.ds((onward // 2) * half, half)]
            copy = remote(part, part, x_send.at[d, onward], x_recv.at[d, onward], to_x[e])
            copy.start()
            copies.append(copy)
    for d in NEAR_FIRST:
        source = (z + 8 - d) % 8
        for onward in (0, 2):
            part = kv_ref.at[core, source, (x + 2) % 4, pl.ds((onward // 2) * half, half)]
            remote(part, part, x_send.at[d, onward], x_recv.at[d, onward], to_x[1]).wait_recv()
        row = kv_ref.at[core, source]
        copy = remote(row, row, p_send.at[d], p_recv.at[d], partner)
        copy.start()
        copies.append(copy)
    for d in NEAR_FIRST:
        row = kv_ref.at[1 - core, (z + 8 - d) % 8]
        remote(row, row, p_send.at[d], p_recv.at[d], partner).wait_recv()
    arrive_rows()
    drain()
    for copy in copies:
        copy.wait_send()


def gather(pack, qd):
    vmem = pl.BlockSpec(memory_space=pltpu.VMEM)
    dma = pltpu.SemaphoreType.DMA
    return pl.pallas_call(
        gather_kernel,
        name="gather",
        out_shape=(
            jax.ShapeDtypeStruct((2, 8, 4, BALANCED_TOKENS, 2 * HEAD_SIZE), pack.dtype),
            jax.ShapeDtypeStruct(qd.shape, qd.dtype),
            jax.ShapeDtypeStruct((8, HEAD_SIZE), jnp.int32),
            jax.ShapeDtypeStruct((2, 8, GROUP * ROWS), jnp.float32),
            jax.ShapeDtypeStruct((1024, BALANCED_TOKENS), pack.dtype),
        ),
        in_specs=[vmem, vmem],
        out_specs=(vmem,) * 5,
        scratch_shapes=[
            pltpu.VMEM(pack.shape, pack.dtype),
            pltpu.VMEM((64, 16, HEAD_SIZE), pack.dtype),
            pltpu.VMEM((64, 16, HEAD_SIZE), pack.dtype),
            pltpu.VMEM((BALANCED_TOKENS, 2 * HEAD_SIZE), pack.dtype),
            dma((4,)), dma((8,)), dma((8,)), dma((8, 4)), dma((8, 4)), dma((8,)), dma((8,)),
            dma((8,)), dma((8,)), dma((8,)), dma((8,)), dma((64,)), dma((64,)),
        ],
        compiler_params=pltpu.CompilerParams(
            collective_id=0, has_side_effects=True, vmem_limit_bytes=20 << 20
        ),
    )(pack, qd)


def reduce_kernel(
    first_ref, pick_ref, kv_ref, dq_ref, grad_ref, rows_ref, from_core, to_row, from_row, to_column,
    from_column, total, to_home, at_home, to_slot, own_sem, p_send, p_recv, x_send, x_recv, z_send,
    z_recv, h_send, h_recv, k_send, k_recv, s_send, s_recv,
):
    z, x, core, head, to_z, to_x, partner, to_head = peers()
    f32 = jnp.float32
    meet((to_head[1:],))
    order = (4, 3, 5, 2, 6, 1, 7, 0)
    copies = []
    for d in order:
        there = (z + d) % 8
        copy = remote(
            kv_ref.at[1 - core, there], from_core.at[there], p_send.at[d], p_recv.at[d], partner
        )
        copy.start()
        copies.append(copy)
    more, arrive_rows = scatter_head(
        dq_ref, rows_ref, head, own_sem.at[0], h_send, h_recv, to_head
    )
    copies = copies + more
    for d in order:
        there = (z + d) % 8
        remote(
            kv_ref.at[1 - core, there], from_core.at[there], p_send.at[d], p_recv.at[d], partner
        ).wait_recv()
        for e in (2, 1, 3):
            other = (x + e) % 4
            to_row[e, d] = (
                kv_ref[core, there, other].astype(f32) + from_core[there, other].astype(f32)
            ).astype(to_row.dtype)
            copy = remote(
                to_row.at[e, d], from_row.at[e, d], x_send.at[e, d], x_recv.at[e, d], to_x[e]
            )
            copy.start()
            copies.append(copy)
    for d in order:
        there = (z + d) % 8
        part = kv_ref[core, there, x].astype(f32) + from_core[there, x].astype(f32)
        for e in (1, 3, 2):
            remote(
                to_row.at[e, d], from_row.at[e, d], x_send.at[e, d], x_recv.at[e, d], to_x[e]
            ).wait_recv()
            part = part + from_row[e, d].astype(f32)
        if d == 0:
            total[...] = part
        else:
            to_column[d] = part.astype(to_column.dtype)
            copy = remote(
                to_column.at[d], from_column.at[d], z_send.at[d], z_recv.at[d], to_z[d]
            )
            copy.start()
            copies.append(copy)
    part = total[...]
    for d in order[:-1]:
        remote(
            to_column.at[d], from_column.at[d], z_send.at[d], z_recv.at[d], to_z[d]
        ).wait_recv()
        part = part + from_column[d].astype(f32)
    i32 = jnp.int32
    bf16 = jnp.bfloat16
    one = jnp.ones((), f32)
    zero = jnp.zeros((), f32)
    part = part.astype(bf16)
    pick = pick_ref[...].astype(f32)
    is_key = (lax.broadcasted_iota(i32, pick.shape, 0) // 8) % 2 == 0
    sent = jnp.dot(
        jnp.where(is_key, pick, zero).astype(bf16), part[:, :HEAD_SIZE], preferred_element_type=f32
    ) + jnp.dot(
        jnp.where(is_key, zero, pick).astype(bf16), part[:, HEAD_SIZE:], preferred_element_type=f32
    )
    to_home[...] = sent.astype(bf16).reshape(64, 16, HEAD_SIZE)
    lands, drain = scatter_seq(to_home, at_home, own_sem.at[1], s_send, s_recv)
    home = to_slot.shape[1]
    shape = (8 * home, 1024)
    slot = lax.broadcasted_iota(i32, shape, 0)
    column = lax.broadcasted_iota(i32, shape, 1)
    wanted = (((slot & 63) + wide(first_ref[0:1, 0:1], shape)) & 63) * 16 + (slot >> 6)
    lands()
    come = at_home[...].reshape(1024, HEAD_SIZE)
    for half in range(2):
        chosen = jnp.where(column == wanted + 8 * half, one, zero).astype(bf16)
        to_slot[:, :, pl.ds(half * HEAD_SIZE, HEAD_SIZE)] = (
            jnp.dot(chosen, come, preferred_element_type=f32)
            .astype(bf16)
            .reshape(8, home, HEAD_SIZE)
        )
    more, arrive = scatter_head(
        to_slot, grad_ref, head, own_sem.at[2], k_send, k_recv, to_head
    )
    copies = copies + more
    arrive_rows()
    arrive()
    drain()
    for copy in copies:
        copy.wait_send()


def reduce(first, pick, dkv, dq):
    vmem = pl.BlockSpec(memory_space=pltpu.VMEM)
    dma = pltpu.SemaphoreType.DMA
    block = dkv.shape[3:]
    bf16 = jnp.bfloat16
    return pl.pallas_call(
        reduce_kernel,
        name="reduce",
        out_shape=(
            jax.ShapeDtypeStruct(dq.shape[:2] + (2 * HEAD_SIZE,), bf16),
            jax.ShapeDtypeStruct(dq.shape, dq.dtype),
        ),
        in_specs=[vmem] * 4,
        out_specs=(vmem, vmem),
        scratch_shapes=[
            pltpu.VMEM((8, 4) + block, bf16),
            pltpu.VMEM((4, 8) + block, bf16),
            pltpu.VMEM((4, 8) + block, bf16),
            pltpu.VMEM((8,) + block, bf16),
            pltpu.VMEM((8,) + block, bf16),
            pltpu.VMEM(block, jnp.float32),
            pltpu.VMEM((64, 16, HEAD_SIZE), bf16),
            pltpu.VMEM((64, 16, HEAD_SIZE), bf16),
            pltpu.VMEM(dq.shape[:2] + (2 * HEAD_SIZE,), bf16),
            dma((3,)), dma((8,)), dma((8,)), dma((4, 8)), dma((4, 8)), dma((8,)), dma((8,)),
            dma((8,)), dma((8,)), dma((8,)), dma((8,)), dma((64,)), dma((64,)),
        ],
        compiler_params=pltpu.CompilerParams(
            collective_id=1, has_side_effects=True, vmem_limit_bytes=24 << 20
        ),
    )(first, pick, dkv, dq)


def per_device(queries, keys, values, outputs, output_gradient, lse, ranks):
    owners = lax.axis_size("seq")
    heads = lax.axis_size("head")
    home_rows = queries.shape[0]
    capacity = home_rows * heads
    survivors = BALANCED_TOKENS * owners
    bf16 = jnp.bfloat16
    width = 2 * HEAD_SIZE

    dots = jnp.sum(
        output_gradient.astype(jnp.float32).reshape(home_rows, QUERY_HEADS, HEAD_SIZE)
        * outputs.astype(jnp.float32).reshape(home_rows, QUERY_HEADS, HEAD_SIZE),
        axis=-1,
    ).astype(bf16)

    def by_head(array):
        return array.reshape(home_rows, heads, -1).transpose(1, 0, 2)

    living = jnp.sum((ranks < survivors).astype(jnp.int32))
    digits = jnp.stack([ranks[0] // 128, ranks[0] % 128, living]).astype(bf16)
    small = jnp.concatenate([by_head(lse), by_head(dots)], axis=-1).transpose(0, 2, 1)
    small = jnp.pad(small, ((0, 0), (0, 0), (0, width - home_rows)))
    digit_rows = jnp.broadcast_to(
        jnp.pad(digits, (0, width - 3))[None, None], (heads, 16 - 2 * GROUP, width)
    )
    first_pack = jnp.concatenate(
        [jnp.concatenate([by_head(keys), by_head(values)], axis=-1), small, digit_rows], axis=1
    )
    all_kv, qd, meta, stats, pick = gather(
        first_pack, jnp.concatenate([by_head(queries), by_head(output_gradient)], axis=-1)
    )
    all_kv = all_kv.reshape(owners, BALANCED_TOKENS, width)
    qd = qd.reshape(capacity, 2 * GROUP * HEAD_SIZE)

    dq, dkv = attention(meta, qd, stats, all_kv)

    back, dq = reduce(
        meta,
        pick,
        dkv.reshape(2, 8, 4, BALANCED_TOKENS, width),
        dq.reshape(heads, home_rows, GROUP * HEAD_SIZE),
    )
    query_grads = dq.transpose(1, 0, 2).reshape(home_rows, -1)
    key_grads = back[:, :, :HEAD_SIZE].transpose(1, 0, 2).reshape(home_rows, -1)
    value_grads = back[:, :, HEAD_SIZE:].transpose(1, 0, 2).reshape(home_rows, -1)
    return (query_grads, key_grads, value_grads)


def solution(mesh):
    placed = P(("seq", "head"), None)
    return jax.shard_map(
        per_device,
        mesh=mesh,
        in_specs=(placed,) * 6 + (P(("seq", "head")),),
        out_specs=(placed,) * 3,
        check_vma=False,
    )
```

```python
import functools

import jax
import jax.numpy as jnp
from jax import lax
from jax.experimental import pallas as pl
from jax.experimental.pallas import tpu as pltpu
from jax.sharding import PartitionSpec as P

QUERY_HEADS = 40
KEY_VALUE_HEADS = 8
HEAD_SIZE = 128
BALANCED_TOKENS = 128
GROUP = QUERY_HEADS // KEY_VALUE_HEADS
LOG2E = 1.4426950408889634
ROWS = 128
BAND = 16
OWNERS = 16


def attention_kernel(
    meta_ref, qd_ref, stat_ref, kv_ref, dq_ref, dkv_ref, q_sc, g_sc, dq_sc, acc
):
    first = meta_ref[0, 0]
    count = meta_ref[0, 1]
    owners = kv_ref.shape[0]
    blocks = q_sc.shape[0]
    stacked = GROUP * ROWS
    chunk = OWNERS * BAND
    scale = HEAD_SIZE ** (-0.5)
    row_span = BAND * owners
    acc[...] = jnp.zeros_like(acc)
    dq_sc[...] = jnp.zeros_like(dq_sc)
    for b in range(blocks):
        live = (lax.broadcasted_iota(jnp.int32, (ROWS, HEAD_SIZE), 0) + b * ROWS) < count
        for m in range(GROUP):
            rows = pl.ds(b * ROWS, ROWS)
            q = qd_ref[rows, pl.ds(m * HEAD_SIZE, HEAD_SIZE)]
            g = qd_ref[rows, pl.ds((GROUP + m) * HEAD_SIZE, HEAD_SIZE)]
            zero = jnp.zeros((), jnp.float32)
            q_sc[b, pl.ds(m * ROWS, ROWS), :] = jnp.where(
                live, q.astype(jnp.float32), zero
            ).astype(jnp.bfloat16)
            g_sc[b, pl.ds(m * ROWS, ROWS), :] = jnp.where(
                live, g.astype(jnp.float32), zero
            ).astype(jnp.bfloat16)
    live_blocks = (count + ROWS - 1) // ROWS
    key_blocks = (first + count + row_span - 1) // row_span
    index = lax.broadcasted_iota(jnp.int32, (chunk, stacked), 0)
    place_in = index // BAND
    key_local = (index % BAND) * owners + (place_in // 4) * 8 + (place_in % 4) * 2
    row_local = lax.broadcasted_iota(jnp.int32, (chunk, stacked), 1) % ROWS
    gap = key_local - row_local

    def key_block(j, carry):
        lowest = jnp.maximum(j * row_span - first, 0) // ROWS
        whole = (jnp.maximum((j + 1) * row_span - 1 - first, 0) + ROWS - 1) // ROWS
        whole = jnp.maximum(jnp.minimum(whole, live_blocks), lowest)
        band = pl.ds(pl.multiple_of(j * BAND, BAND), BAND)
        for c in range(owners // OWNERS):
            own = pl.ds(c * OWNERS, OWNERS)
            key = kv_ref[own, band, pl.ds(0, HEAD_SIZE)].reshape(chunk, HEAD_SIZE)
            value = kv_ref[own, band, pl.ds(HEAD_SIZE, HEAD_SIZE)].reshape(chunk, HEAD_SIZE)
            key_t = key.astype(jnp.float32).T.astype(jnp.bfloat16)

            def row_block(b, inner, masked):
                q = q_sc[b]
                g = g_sc[b]
                nt = (((1,), (1,)), ((), ()))
                nn = (((1,), (0,)), ((), ()))
                f32 = jnp.float32
                score = lax.dot_general(key, q, nt, preferred_element_type=f32)
                dprob = lax.dot_general(value, g, nt, preferred_element_type=f32)
                limit = first + b * ROWS - j * row_span - (c % 2) * 32 - c // 2
                prob = jnp.exp2(score * (scale * LOG2E) - stat_ref[0, pl.ds(b, 1), :])
                if masked:
                    prob = jnp.where(gap <= limit, prob, 0.0)
                dscore = prob * (dprob - stat_ref[1, pl.ds(b, 1), :])
                prob_low = prob.astype(jnp.bfloat16)
                dscore_low = dscore.astype(jnp.bfloat16)
                dk = lax.dot_general(dscore_low, q, nn, preferred_element_type=f32)
                dv = lax.dot_general(prob_low, g, nn, preferred_element_type=f32)
                acc[own, band, pl.ds(0, HEAD_SIZE)] += dk.reshape(OWNERS, BAND, HEAD_SIZE)
                acc[own, band, pl.ds(HEAD_SIZE, HEAD_SIZE)] += dv.reshape(OWNERS, BAND, HEAD_SIZE)
                dq_sc[b] += lax.dot_general(key_t, dscore_low, nn, preferred_element_type=f32)
                return inner

            lax.fori_loop(lowest, whole, functools.partial(row_block, masked=True), 0)
            lax.fori_loop(whole, live_blocks, functools.partial(row_block, masked=False), 0)
        return carry

    lax.fori_loop(0, key_blocks, key_block, 0)
    for b in range(blocks):
        for m in range(GROUP):
            part = dq_sc[b, :, pl.ds(m * ROWS, ROWS)].T * scale
            dq_ref[pl.ds(b * ROWS, ROWS), pl.ds(m * HEAD_SIZE, HEAD_SIZE)] = part.astype(
                dq_ref.dtype
            )
    dkv_ref[:, :, pl.ds(0, HEAD_SIZE)] = (acc[:, :, pl.ds(0, HEAD_SIZE)] * scale).astype(
        dkv_ref.dtype
    )
    dkv_ref[:, :, pl.ds(HEAD_SIZE, HEAD_SIZE)] = acc[:, :, pl.ds(HEAD_SIZE, HEAD_SIZE)].astype(
        dkv_ref.dtype
    )


def attention(meta, qd, stats, kv, interpret=False):
    capacity = qd.shape[0]
    owners, per_owner, width = kv.shape
    blocks = capacity // ROWS
    vmem = pl.BlockSpec(memory_space=pltpu.VMEM)
    return pl.pallas_call(
        attention_kernel,
        name="attention",
        out_shape=(
            jax.ShapeDtypeStruct((capacity, GROUP * HEAD_SIZE), jnp.bfloat16),
            jax.ShapeDtypeStruct(kv.shape, jnp.bfloat16),
        ),
        in_specs=[pl.BlockSpec(memory_space=pltpu.SMEM), vmem, vmem, vmem],
        out_specs=(vmem, vmem),
        scratch_shapes=[
            pltpu.VMEM((blocks, GROUP * ROWS, HEAD_SIZE), jnp.bfloat16),
            pltpu.VMEM((blocks, GROUP * ROWS, HEAD_SIZE), jnp.bfloat16),
            pltpu.VMEM((blocks, HEAD_SIZE, GROUP * ROWS), jnp.float32),
            pltpu.VMEM(kv.shape, jnp.float32),
        ],
        compiler_params=pltpu.CompilerParams(vmem_limit_bytes=26 << 20),
        cost_estimate=pl.CostEstimate(
            flops=10 * capacity * GROUP * HEAD_SIZE * owners * per_owner // 2,
            bytes_accessed=2 * (2 * kv.size + 3 * qd.size),
            transcendentals=0,
        ),
        interpret=interpret,
    )(meta, qd, stats, kv)


def place(seq_index):
    return seq_index // 8, (seq_index // 2) % 4, seq_index % 2


def peers():
    seq = lax.axis_index("seq")
    head = lax.axis_index("head")
    z, x, core = place(seq)
    spot = lambda z, x, core: (z * 8 + x * 2 + core, head)
    to_z = [None] + [spot((z + d) % 8, x, core) for d in range(1, 8)]
    to_x = [None] + [spot(z, (x + e) % 4, core) for e in range(1, 4)]
    partner = spot(z, x, 1 - core)
    to_head = [None] + [(seq, (head + d) % 8) for d in range(1, 8)]
    return z, x, core, head, to_z, to_x, partner, to_head


def meet(groups):
    barrier = pltpu.get_barrier_semaphore()
    seq = lax.axis_index("seq")
    head = lax.axis_index("head")

    def greet(k, carry):
        pl.semaphore_signal(
            barrier,
            inc=1,
            device_id=((seq + k) % 64, head),
            device_id_type=pl.DeviceIdType.MESH,
        )
        return carry

    lax.fori_loop(1, 64, greet, 0)
    total = 63
    for group in groups:
        for device in group:
            pl.semaphore_signal(
                barrier, inc=1, device_id=device, device_id_type=pl.DeviceIdType.MESH
            )
            total += 1
    pl.semaphore_wait(barrier, total)


def remote(src, dst, send, recv, device):
    return pltpu.make_async_remote_copy(
        src_ref=src,
        dst_ref=dst,
        send_sem=send,
        recv_sem=recv,
        device_id=device,
        device_id_type=pl.DeviceIdType.MESH,
    )


def scatter_seq(out_ref, in_ref, own_sem, send, recv):
    seq = lax.axis_index("seq")
    head = lax.axis_index("head")
    own = pltpu.make_async_copy(out_ref.at[seq], in_ref.at[seq], own_sem)
    own.start()

    def copy(k):
        there = (seq + k) % 64
        return remote(
            out_ref.at[there], in_ref.at[seq], send.at[k], recv.at[k], (there, head)
        )

    def start(k, carry):
        copy(k).start()
        return carry

    def finish(k, carry):
        from_there = in_ref.at[(seq + 64 - k) % 64]
        arrived = remote(
            from_there, from_there, send.at[k], recv.at[k], ((seq + k) % 64, head)
        )
        arrived.wait_recv()
        return carry

    def sent(k, carry):
        copy(k).wait_send()
        return carry

    def lands():
        lax.fori_loop(1, 64, finish, 0)
        own.wait()

    lax.fori_loop(1, 64, start, 0)
    return lands, lambda: lax.fori_loop(1, 64, sent, 0)


def scatter_head(out_ref, in_ref, head, own_sem, send, recv, to_head):
    copies = []
    for d in NEAR_FIRST[1:]:
        copy = remote(
            out_ref.at[(head + d) % 8], in_ref.at[head], send.at[d], recv.at[d], to_head[d]
        )
        copy.start()
        copies.append(copy)
    own = pltpu.make_async_copy(out_ref.at[head], in_ref.at[head], own_sem)
    own.start()

    def finish():
        for d in NEAR_FIRST[1:]:
            part = in_ref.at[(head + 8 - d) % 8]
            remote(part, part, send.at[d], recv.at[d], to_head[d]).wait_recv()
        own.wait()

    return copies, finish


def wide(value, shape):
    return jnp.broadcast_to(value, shape)


NEAR_FIRST = (0, 1, 7, 2, 6, 3, 5, 4)


def gather_kernel(
    pack_ref, qd_ref, kv_ref, rows_ref, meta_ref, stat_ref, pick_ref, got_ref, to_owner, at_owner,
    own_ref, own_sem,
    z_send, z_recv, x_send, x_recv, p_send, p_recv, h_send, h_recv, k_send, k_recv, s_send, s_recv,
):
    z, x, core, head, to_z, to_x, partner, to_head = peers()
    f32 = jnp.float32
    i32 = jnp.int32
    bf16 = jnp.bfloat16
    meet((to_head[1:],))
    copies, arrive = scatter_head(
        pack_ref, got_ref, head, own_sem.at[0], k_send, k_recv, to_head
    )
    arrive()
    more, arrive_rows = scatter_head(
        qd_ref, rows_ref, head, own_sem.at[1], h_send, h_recv, to_head
    )
    copies = copies + more
    home = got_ref.shape[1] - 16
    capacity = 8 * home
    slots = capacity // 64
    notes = got_ref[0, pl.ds(home, 16), :].astype(f32)
    first = (notes[10:11, 0:1] * 128 + notes[10:11, 1:2]).astype(i32)
    count = notes[10:11, 2:3]
    for h in range(1, 8):
        count = count + got_ref[h, pl.ds(home, 16), :].astype(f32)[10:11, 2:3]
    count = count.astype(i32)
    shape = (1024, capacity)
    row = lax.broadcasted_iota(i32, shape, 0)
    column = lax.broadcasted_iota(i32, shape, 1)
    wanted = (row % 8) * 64 + ((row // 16 - wide(first, shape)) & 63)
    hit = (column == wanted) & (row % 8 < slots)
    is_key = (row // 8) % 2 == 0
    one = jnp.ones((), f32)
    zero = jnp.zeros((), f32)
    take_key = jnp.where(hit & is_key, one, zero).astype(bf16)
    take_value = jnp.where(hit & ~is_key, one, zero).astype(bf16)
    pairs = got_ref[:, pl.ds(0, home), :].reshape(capacity, 2 * HEAD_SIZE)
    sent = jnp.dot(take_key, pairs[:, :HEAD_SIZE], preferred_element_type=f32) + jnp.dot(
        take_value, pairs[:, HEAD_SIZE:], preferred_element_type=f32
    )
    shape = (1024, HEAD_SIZE)
    row = lax.broadcasted_iota(i32, shape, 0)
    lane = lax.broadcasted_iota(i32, shape, 1)
    first_wide = wide(first, shape)
    count_wide = wide(count, shape)
    note = jnp.where(
        lane == 0,
        first_wide >> 7,
        jnp.where(
            lane == 1,
            first_wide & 127,
            jnp.where(lane == 2, count_wide >> 7, jnp.where(lane == 3, count_wide & 127, 0)),
        ),
    ).astype(f32)
    sent = jnp.where(row % 16 == slots, note, sent)
    to_owner[...] = sent.astype(bf16).reshape(64, 16, HEAD_SIZE)
    lands, drain = scatter_seq(to_owner, at_owner, own_sem.at[2], s_send, s_recv)
    shape = meta_ref.shape
    lane_of = lax.broadcasted_iota(i32, shape, 1)
    meta_ref[...] = jnp.where(
        lane_of == 0, wide(first, shape), jnp.where(lane_of == 1, wide(count, shape), 0)
    )
    shape = (2 * HEAD_SIZE, capacity)
    apart = lax.broadcasted_iota(i32, shape, 1) - lax.broadcasted_iota(i32, shape, 0)
    inside = lax.broadcasted_iota(i32, shape, 0) < home
    stats = jnp.zeros((16, capacity), f32)
    for h in range(8):
        spread = jnp.where(inside & (apart == h * home), one, zero).astype(bf16)
        stats = stats + jnp.dot(
            got_ref[h, pl.ds(home, 16), :], spread, preferred_element_type=f32
        )
    slot = lax.broadcasted_iota(i32, stats.shape, 1)
    stats = jnp.where(slot < wide(count, stats.shape), stats, 0.0)
    for b in range(capacity // ROWS):
        for m in range(GROUP):
            lanes = pl.ds(m * ROWS, ROWS)
            part = stats[:, b * ROWS : (b + 1) * ROWS]
            stat_ref[0, pl.ds(b, 1), lanes] = part[m : m + 1] * LOG2E
            stat_ref[1, pl.ds(b, 1), lanes] = part[GROUP + m : GROUP + m + 1]
    shape = (1024, HEAD_SIZE)
    lands()
    come = at_owner[...].reshape(1024, HEAD_SIZE)
    told = come.astype(f32).reshape(64, 16, HEAD_SIZE)[:, slots : slots + 1, :]
    told = wide(told, (64, 16, HEAD_SIZE)).reshape(1024, HEAD_SIZE)
    starts = wide((told[:, 0:1] * 128 + told[:, 1:2]).astype(i32), shape)
    counts = wide((told[:, 2:3] * 128 + told[:, 3:4]).astype(i32), shape)
    turn = row % 8
    within = turn * 64 + ((lax.axis_index("seq") - starts) & 63)
    alive = (within < counts) & (turn < slots)
    target = jnp.where(alive, (starts + within) >> 6, -1)
    pick = jnp.where(target == lane, one, zero)
    pick_ref[...] = pick.astype(bf16)
    is_key = (row // 8) % 2 == 0
    for half in range(2):
        chosen = jnp.where(is_key if half == 0 else ~is_key, pick, zero).T.astype(bf16)
        own_ref[:, pl.ds(half * HEAD_SIZE, HEAD_SIZE)] = jnp.dot(
            chosen, come, preferred_element_type=f32
        ).astype(bf16)
    for d in NEAR_FIRST[1:]:
        copy = remote(own_ref, kv_ref.at[core, z, x], z_send.at[d], z_recv.at[d], to_z[d])
        copy.start()
        copies.append(copy)
    mine = pltpu.make_async_copy(own_ref, kv_ref.at[core, z, x], own_sem.at[3])
    mine.start()
    for d in NEAR_FIRST:
        source = (z + 8 - d) % 8
        block = kv_ref.at[core, source, x]
        if d == 0:
            mine.wait()
        else:
            remote(own_ref, block, z_send.at[d], z_recv.at[d], to_z[d]).wait_recv()
        for e in (1, 3):
            copy = remote(block, block, x_send.at[d, e], x_recv.at[d, e], to_x[e])
            copy.start()
            copies.append(copy)
    half = BALANCED_TOKENS // 2
    for d in NEAR_FIRST:
        source = (z + 8 - d) % 8
        for e, onward in ((1, 0), (3, 2)):
            block = kv_ref.at[core, source, (x + 4 - e) % 4]
            remote(block, block, x_send.at[d, e], x_recv.at[d, e], to_x[e]).wait_recv()
            part = block.at[pl.ds((onward // 2) * half, half)]
            copy = remote(part, part, x_send.at[d, onward], x_recv.at[d, onward], to_x[e])
            copy.start()
            copies.append(copy)
    for d in NEAR_FIRST:
        source = (z + 8 - d) % 8
        for onward in (0, 2):
            part = kv_ref.at[core, source, (x + 2) % 4, pl.ds((onward // 2) * half, half)]
            remote(part, part, x_send.at[d, onward], x_recv.at[d, onward], to_x[1]).wait_recv()
        row = kv_ref.at[core, source]
        copy = remote(row, row, p_send.at[d], p_recv.at[d], partner)
        copy.start()
        copies.append(copy)
    for d in NEAR_FIRST:
        row = kv_ref.at[1 - core, (z + 8 - d) % 8]
        remote(row, row, p_send.at[d], p_recv.at[d], partner).wait_recv()
    arrive_rows()
    drain()
    for copy in copies:
        copy.wait_send()


def gather(pack, qd):
    vmem = pl.BlockSpec(memory_space=pltpu.VMEM)
    dma = pltpu.SemaphoreType.DMA
    return pl.pallas_call(
        gather_kernel,
        name="gather",
        out_shape=(
            jax.ShapeDtypeStruct((2, 8, 4, BALANCED_TOKENS, 2 * HEAD_SIZE), pack.dtype),
            jax.ShapeDtypeStruct(qd.shape, qd.dtype),
            jax.ShapeDtypeStruct((8, HEAD_SIZE), jnp.int32),
            jax.ShapeDtypeStruct((2, 8, GROUP * ROWS), jnp.float32),
            jax.ShapeDtypeStruct((1024, BALANCED_TOKENS), pack.dtype),
        ),
        in_specs=[vmem, vmem],
        out_specs=(vmem,) * 5,
        scratch_shapes=[
            pltpu.VMEM(pack.shape, pack.dtype),
            pltpu.VMEM((64, 16, HEAD_SIZE), pack.dtype),
            pltpu.VMEM((64, 16, HEAD_SIZE), pack.dtype),
            pltpu.VMEM((BALANCED_TOKENS, 2 * HEAD_SIZE), pack.dtype),
            dma((4,)), dma((8,)), dma((8,)), dma((8, 4)), dma((8, 4)), dma((8,)), dma((8,)),
            dma((8,)), dma((8,)), dma((8,)), dma((8,)), dma((64,)), dma((64,)),
        ],
        compiler_params=pltpu.CompilerParams(
            collective_id=0, has_side_effects=True, vmem_limit_bytes=20 << 20
        ),
    )(pack, qd)


def reduce_kernel(
    first_ref, pick_ref, kv_ref, dq_ref, grad_ref, rows_ref, from_core, to_row, from_row, to_column,
    from_column, total, to_home, at_home, to_slot, own_sem, p_send, p_recv, x_send, x_recv, z_send,
    z_recv, h_send, h_recv, k_send, k_recv, s_send, s_recv,
):
    z, x, core, head, to_z, to_x, partner, to_head = peers()
    f32 = jnp.float32
    meet((to_head[1:],))
    order = (4, 3, 5, 2, 6, 1, 7, 0)
    copies = []
    for d in order:
        there = (z + d) % 8
        copy = remote(
            kv_ref.at[1 - core, there], from_core.at[there], p_send.at[d], p_recv.at[d], partner
        )
        copy.start()
        copies.append(copy)
    more, arrive_rows = scatter_head(
        dq_ref, rows_ref, head, own_sem.at[0], h_send, h_recv, to_head
    )
    copies = copies + more
    for d in order:
        there = (z + d) % 8
        remote(
            kv_ref.at[1 - core, there], from_core.at[there], p_send.at[d], p_recv.at[d], partner
        ).wait_recv()
        for e in (2, 1, 3):
            other = (x + e) % 4
            to_row[e, d] = (
                kv_ref[core, there, other].astype(f32) + from_core[there, other].astype(f32)
            ).astype(to_row.dtype)
            copy = remote(
                to_row.at[e, d], from_row.at[e, d], x_send.at[e, d], x_recv.at[e, d], to_x[e]
            )
            copy.start()
            copies.append(copy)
    for d in order:
        there = (z + d) % 8
        part = kv_ref[core, there, x].astype(f32) + from_core[there, x].astype(f32)
        for e in (1, 3, 2):
            remote(
                to_row.at[e, d], from_row.at[e, d], x_send.at[e, d], x_recv.at[e, d], to_x[e]
            ).wait_recv()
            part = part + from_row[e, d].astype(f32)
        if d == 0:
            total[...] = part
        else:
            to_column[d] = part.astype(to_column.dtype)
            copy = remote(
                to_column.at[d], from_column.at[d], z_send.at[d], z_recv.at[d], to_z[d]
            )
            copy.start()
            copies.append(copy)
    part = total[...]
    for d in order[:-1]:
        remote(
            to_column.at[d], from_column.at[d], z_send.at[d], z_recv.at[d], to_z[d]
        ).wait_recv()
        part = part + from_column[d].astype(f32)
    i32 = jnp.int32
    bf16 = jnp.bfloat16
    one = jnp.ones((), f32)
    zero = jnp.zeros((), f32)
    part = part.astype(bf16)
    pick = pick_ref[...].astype(f32)
    is_key = (lax.broadcasted_iota(i32, pick.shape, 0) // 8) % 2 == 0
    sent = jnp.dot(
        jnp.where(is_key, pick, zero).astype(bf16), part[:, :HEAD_SIZE], preferred_element_type=f32
    ) + jnp.dot(
        jnp.where(is_key, zero, pick).astype(bf16), part[:, HEAD_SIZE:], preferred_element_type=f32
    )
    to_home[...] = sent.astype(bf16).reshape(64, 16, HEAD_SIZE)
    lands, drain = scatter_seq(to_home, at_home, own_sem.at[1], s_send, s_recv)
    home = to_slot.shape[1]
    shape = (8 * home, 1024)
    slot = lax.broadcasted_iota(i32, shape, 0)
    column = lax.broadcasted_iota(i32, shape, 1)
    wanted = (((slot & 63) + wide(first_ref[0:1, 0:1], shape)) & 63) * 16 + (slot >> 6)
    lands()
    come = at_home[...].reshape(1024, HEAD_SIZE)
    for half in range(2):
        chosen = jnp.where(column == wanted + 8 * half, one, zero).astype(bf16)
        to_slot[:, :, pl.ds(half * HEAD_SIZE, HEAD_SIZE)] = (
            jnp.dot(chosen, come, preferred_element_type=f32)
            .astype(bf16)
            .reshape(8, home, HEAD_SIZE)
        )
    more, arrive = scatter_head(
        to_slot, grad_ref, head, own_sem.at[2], k_send, k_recv, to_head
    )
    copies = copies + more
    arrive_rows()
    arrive()
    drain()
    for copy in copies:
        copy.wait_send()


def reduce(first, pick, dkv, dq):
    vmem = pl.BlockSpec(memory_space=pltpu.VMEM)
    dma = pltpu.SemaphoreType.DMA
    block = dkv.shape[3:]
    bf16 = jnp.bfloat16
    return pl.pallas_call(
        reduce_kernel,
        name="reduce",
        out_shape=(
            jax.ShapeDtypeStruct(dq.shape[:2] + (2 * HEAD_SIZE,), bf16),
            jax.ShapeDtypeStruct(dq.shape, dq.dtype),
        ),
        in_specs=[vmem] * 4,
        out_specs=(vmem, vmem),
        scratch_shapes=[
            pltpu.VMEM((8, 4) + block, bf16),
            pltpu.VMEM((4, 8) + block, bf16),
            pltpu.VMEM((4, 8) + block, bf16),
            pltpu.VMEM((8,) + block, bf16),
            pltpu.VMEM((8,) + block, bf16),
            pltpu.VMEM(block, jnp.float32),
            pltpu.VMEM((64, 16, HEAD_SIZE), bf16),
            pltpu.VMEM((64, 16, HEAD_SIZE), bf16),
            pltpu.VMEM(dq.shape[:2] + (2 * HEAD_SIZE,), bf16),
            dma((3,)), dma((8,)), dma((8,)), dma((4, 8)), dma((4, 8)), dma((8,)), dma((8,)),
            dma((8,)), dma((8,)), dma((8,)), dma((8,)), dma((64,)), dma((64,)),
        ],
        compiler_params=pltpu.CompilerParams(
            collective_id=1, has_side_effects=True, vmem_limit_bytes=24 << 20
        ),
    )(first, pick, dkv, dq)


def per_device(queries, keys, values, outputs, output_gradient, lse, ranks):
    owners = lax.axis_size("seq")
    heads = lax.axis_size("head")
    home_rows = queries.shape[0]
    capacity = home_rows * heads
    survivors = BALANCED_TOKENS * owners
    bf16 = jnp.bfloat16
    width = 2 * HEAD_SIZE

    dots = jnp.sum(
        output_gradient.astype(jnp.float32).reshape(home_rows, QUERY_HEADS, HEAD_SIZE)
        * outputs.astype(jnp.float32).reshape(home_rows, QUERY_HEADS, HEAD_SIZE),
        axis=-1,
    ).astype(bf16)

    def by_head(array):
        return array.reshape(home_rows, heads, -1).transpose(1, 0, 2)

    living = jnp.sum((ranks < survivors).astype(jnp.int32))
    digits = jnp.stack([ranks[0] // 128, ranks[0] % 128, living]).astype(bf16)
    small = jnp.concatenate([by_head(lse), by_head(dots)], axis=-1).transpose(0, 2, 1)
    small = jnp.pad(small, ((0, 0), (0, 0), (0, width - home_rows)))
    digit_rows = jnp.broadcast_to(
        jnp.pad(digits, (0, width - 3))[None, None], (heads, 16 - 2 * GROUP, width)
    )
    first_pack = jnp.concatenate(
        [jnp.concatenate([by_head(keys), by_head(values)], axis=-1), small, digit_rows], axis=1
    )
    all_kv, qd, meta, stats, pick = gather(
        first_pack, jnp.concatenate([by_head(queries), by_head(output_gradient)], axis=-1)
    )
    all_kv = all_kv.reshape(owners, BALANCED_TOKENS, width)
    qd = qd.reshape(capacity, 2 * GROUP * HEAD_SIZE)

    dq, dkv = attention(meta, qd, stats, all_kv)

    back, dq = reduce(
        meta,
        pick,
        dkv.reshape(2, 8, 4, BALANCED_TOKENS, width),
        dq.reshape(heads, home_rows, GROUP * HEAD_SIZE),
    )
    query_grads = dq.transpose(1, 0, 2).reshape(home_rows, -1)
    key_grads = back[:, :, :HEAD_SIZE].transpose(1, 0, 2).reshape(home_rows, -1)
    value_grads = back[:, :, HEAD_SIZE:].transpose(1, 0, 2).reshape(home_rows, -1)
    return (query_grads, key_grads, value_grads)


def solution(mesh):
    placed = P(("seq", "head"), None)
    return jax.shard_map(
        per_device,
        mesh=mesh,
        in_specs=(placed,) * 6 + (P(("seq", "head")),),
        out_specs=(placed,) * 3,
        check_vma=False,
    )
```
